256 devices in a mesh: dp: 8 (over z), seq: 32 (over x, y, core).
Axes of the slice: x: 4, y: 4, z: 8, core: 2. Of those that a mesh axis runs over, the one named last changes fastest.
Arguments:
- tokens: bfloat16 [16384, 4096], P('seq', 'dp'), may hold values from -6 to 6
- weights: bfloat16 [4096, 3, 2048], P('seq', None, 'dp'), may hold values from -0.1875 to 0.1875
- log_decay: float32 [16, 16384], P('dp', 'seq'), may hold values from -1.6 to 0, as said below
- cotangent: bfloat16 [16384, 2048], P('seq', 'dp'), may hold values from -6 to 6
Outputs:
- attended: bfloat16 [16384, 2048], P('seq', 'dp')
- grad_tokens: bfloat16 [16384, 4096], P('seq', 'dp')
- grad_weights: bfloat16 [4096, 3, 2048], P('seq', None, 'dp')
The draws below stay inside these ranges and needn't reach their ends.
Inputs may be any that keep to these rules, and one draw needn't show every extreme that they name: `log_decay`: log of the share of each head's state kept at each token.
All inputs are finite; a program needn't handle non-finite values.
Results may differ from the reference program's by a relative error of at most 0.015.
Values may be sent and summed in bfloat16 or wider, within the bound.
A program may use at most 64 MiB of HBM per device.

```python
import math
import jax
import jax.numpy as jnp
from jax import lax

D = 4096
HALF_HEAD_COUNT = 16
HD = 128
TOK_DEV = 512
SEQUENCE_TOKENS = 16384
N_SEQ = 32


def draw_log_decay(key, part):
    parallel_lanes = jax.random.split(key, 7)
    order = jax.random.permutation(parallel_lanes[0], HALF_HEAD_COUNT)
    quick = order < HALF_HEAD_COUNT // 2
    quick_rate = jnp.exp(jax.random.uniform(parallel_lanes[1], (HALF_HEAD_COUNT,), jnp.float32, math.log(1.0 / 60.0), math.log(1.0 / 30.0)))
    slow_rate = jnp.exp(jax.random.uniform(parallel_lanes[2], (HALF_HEAD_COUNT,), jnp.float32, math.log(0.05), math.log(0.3))) / SEQUENCE_TOKENS
    baseline_decay_rate = jnp.where(quick, quick_rate, slow_rate)
    shard_multiplier = jnp.exp(jax.random.uniform(parallel_lanes[3], (HALF_HEAD_COUNT, SEQUENCE_TOKENS // TOK_DEV), jnp.float32, math.log(0.5), math.log(2.0)))
    shard_multiplier = jnp.repeat(shard_multiplier, TOK_DEV, axis=1)
    token_multiplier = jnp.exp(jax.random.uniform(parallel_lanes[4], (HALF_HEAD_COUNT, SEQUENCE_TOKENS), jnp.float32, math.log(0.5), math.log(2.0)))
    group_offsets = jax.random.randint(parallel_lanes[5], (HALF_HEAD_COUNT, 2), 0, SEQUENCE_TOKENS)
    group_depth = jax.random.uniform(parallel_lanes[6], (HALF_HEAD_COUNT, 2), jnp.float32, 0.22, 0.69)
    token_positions = jnp.arange(SEQUENCE_TOKENS)
    token_groups = jnp.sum(jnp.where(token_positions[None, None, :] == group_offsets[:, :, None], group_depth[:, :, None], 0.0), axis=1)
    return -(baseline_decay_rate[:, None] * shard_multiplier * token_multiplier + token_groups)


def raised(result, own_key, source, target, shards_of, factor):
    owner, partner = [(jnp.arange(result.shape[axis_at]) // (result.shape[axis_at] // shards_of)).reshape([-1 if axis == axis_at else 1 for axis in range(result.ndim)]) for axis_at in (source, target)]
    chosen = jax.random.permutation(own_key, shards_of)[partner]
    strong = (owner == chosen) | (owner == (partner + shards_of // 2) % shards_of)
    return jnp.where(strong, factor * result, result)


def block_levels(key, shape, shards, low, largest):
    loudness = 1.0
    for position, blocks in shards:
        draws = jax.random.uniform(jax.random.fold_in(jax.random.fold_in(key, 6), position), (blocks,), jnp.float32, low / len(shards), largest / len(shards))
        loudness = loudness * jnp.repeat(jnp.exp(draws), shape[position] // blocks).reshape((-1,) + (1,) * (len(shape) - 1 - position))
    return loudness


def normal_values(rng, dims, deviation, bound, pieces=(), kind=jnp.bfloat16):
    values = jax.random.normal(rng, dims, jnp.float32) * deviation
    if len(pieces) > 0:
        values = block_levels(rng, dims, pieces, -0.22, 0.18) * values
    return jnp.clip(values, min=-bound, max=bound).astype(kind)


def bell_draw_with(key, dims, scale, reach, shards, heavy, held_as=jnp.bfloat16):
    drawn = scale * jax.random.normal(key, dims, jnp.float32)
    if shards:
        drawn = drawn * block_levels(key, dims, shards, -0.22, 0.18)
    return jnp.clip(raised(drawn, jax.random.fold_in(key, 3), *heavy), -reach, reach).astype(held_as)


def setup_inputs(seed: int = 0) -> dict:
    seeds = jax.random.split(jax.random.key(seed), 5)
    tokens = bell_draw_with(seeds[0], (SEQUENCE_TOKENS, D), 1.0, 6.0, ((0, 32), (1, 8)), (0, 1, 32, 2.75))
    weights = bell_draw_with(seeds[1], (D, 3, HALF_HEAD_COUNT * HD), D ** -0.5, 0.1875, ((0, 32), (2, 8)), (2, 0, 32, 2.75))
    log_decay = draw_log_decay(jax.random.fold_in(seeds[4], 71), 0)
    cotangent = normal_values(seeds[3], (SEQUENCE_TOKENS, HALF_HEAD_COUNT * HD), 1.0, 6.0, ((0, 32), (1, 8)))
    return dict(tokens=tokens, weights=weights, log_decay=log_decay, cotangent=cotangent)


HIGHEST = lax.Precision.HIGHEST
EPSILON = 1e-06

def causal_weights(decay_log):
    running = jnp.cumsum(decay_log, axis=1)
    length = decay_log.shape[1]
    token_positions = jnp.arange(length)
    lower_part = token_positions[:, None] >= token_positions[None, :]
    spread = running[:, :, None] - running[:, None, :]
    mixing = jnp.exp(jnp.where(lower_part[None], spread, -jnp.inf))
    return (running, mixing)

def forward_block(queries, keys_in, values_in, decay_log, carried):
    running, mixing = causal_weights(decay_log)
    scores = jnp.einsum('htd,hjd->htj', queries, keys_in, precision=HIGHEST) * mixing
    inside = jnp.einsum('htj,hje->hte', scores, values_in, precision=HIGHEST)
    outside = jnp.exp(running)[:, :, None] * jnp.einsum('htd,hde->hte', queries, carried, precision=HIGHEST)
    totals = running[:, -1]
    fading = jnp.exp(totals[:, None] - running)[:, :, None]
    summary = jnp.einsum('hjd,hje->hde', keys_in * fading, values_in, precision=HIGHEST)
    return (inside + outside, totals, summary)

def backward_block(queries, keys_in, values_in, decay_log, grad_out, carried, future):
    running, mixing = causal_weights(decay_log)
    totals = running[:, -1]
    scores = jnp.einsum('htd,hjd->htj', queries, keys_in, precision=HIGHEST) * mixing
    through = jnp.einsum('hte,hje->htj', grad_out, values_in, precision=HIGHEST) * mixing
    leading = jnp.exp(running)[:, :, None]
    fading = jnp.exp(totals[:, None] - running)[:, :, None]
    grad_query = jnp.einsum('htj,hjd->htd', through, keys_in, precision=HIGHEST) + leading * jnp.einsum('hte,hde->htd', grad_out, carried, precision=HIGHEST)
    grad_key = jnp.einsum('htj,htd->hjd', through, queries, precision=HIGHEST) + fading * jnp.einsum('hje,hde->hjd', values_in, future, precision=HIGHEST)
    grad_value = jnp.einsum('htj,hte->hje', scores, grad_out, precision=HIGHEST) + fading * jnp.einsum('hjd,hde->hje', keys_in, future, precision=HIGHEST)
    summary = jnp.einsum('htd,hte->hde', queries * leading, grad_out, precision=HIGHEST)
    return (grad_query, grad_key, grad_value, totals, summary)

def silu_slope(values_pre):
    sigmoid_part = jax.nn.sigmoid(values_pre)
    return sigmoid_part * (1.0 + values_pre * (1.0 - sigmoid_part))

def reference(tokens, weights, log_decay, cotangent):
    flat_weights = weights.reshape(D, 3 * HALF_HEAD_COUNT * HD)
    projected = jnp.dot(tokens, flat_weights, preferred_element_type=jnp.float32).reshape(SEQUENCE_TOKENS, 3, HALF_HEAD_COUNT * HD)
    activated = jnp.stack([jax.nn.silu(projected[:, 0]), jax.nn.silu(projected[:, 1]), projected[:, 2]], axis=1).astype(jnp.bfloat16)
    activated = lax.optimization_barrier(activated)

    def to_blocks(matrix):
        return matrix.astype(jnp.float32).reshape(N_SEQ, TOK_DEV, HALF_HEAD_COUNT, HD).transpose(0, 2, 1, 3)

    def from_blocks(matrix):
        return matrix.transpose(0, 2, 1, 3).reshape(SEQUENCE_TOKENS, HALF_HEAD_COUNT * HD)
    queries = to_blocks(activated[:, 0])
    keys_in = to_blocks(activated[:, 1])
    values_in = to_blocks(activated[:, 2])
    decays = log_decay.reshape(HALF_HEAD_COUNT, N_SEQ, TOK_DEV).transpose(1, 0, 2)
    zero_state = jnp.zeros((HALF_HEAD_COUNT, HD, HD), jnp.float32)

    def forward_step(carried, item):
        query_b, key_b, value_b, decay_b = item
        output, totals, summary = forward_block(query_b, key_b, value_b, decay_b, carried)
        return (jnp.exp(totals)[:, None, None] * carried + summary, (output, carried))
    _, (attention, states) = lax.scan(forward_step, zero_state, (queries, keys_in, values_in, decays))
    scale_rms = jnp.sqrt(lax.optimization_barrier(jnp.mean(attention * attention, axis=-1, keepdims=True)) + EPSILON)
    normed = attention / scale_rms
    attended = from_blocks(normed).astype(jnp.bfloat16)
    upstream = to_blocks(cotangent)
    grad_out = (upstream - normed * lax.optimization_barrier(jnp.mean(upstream * normed, axis=-1, keepdims=True))) / scale_rms

    def backward_step(future, item):
        query_b, key_b, value_b, decay_b, grad_b, state_b = item
        grad_query, grad_key, grad_value, totals, summary = backward_block(query_b, key_b, value_b, decay_b, grad_b, state_b, future)
        return (summary + jnp.exp(totals)[:, None, None] * future, (grad_query, grad_key, grad_value))
    _, (grad_query, grad_key, grad_value) = lax.scan(backward_step, zero_state, (queries, keys_in, values_in, decays, grad_out, states), reverse=True)
    grad_pre = jnp.stack([from_blocks(grad_query) * silu_slope(projected[:, 0]), from_blocks(grad_key) * silu_slope(projected[:, 1]), from_blocks(grad_value)], axis=1).astype(jnp.bfloat16)
    grad_flat = grad_pre.reshape(SEQUENCE_TOKENS, 3 * HALF_HEAD_COUNT * HD)
    grad_tokens = jnp.dot(grad_flat, flat_weights.T, preferred_element_type=jnp.float32).astype(jnp.bfloat16)

    def weight_step(accumulated, item):
        token_rows, grad_rows = item
        partial_w = jnp.dot(token_rows.T, grad_rows, preferred_element_type=jnp.float32).astype(jnp.bfloat16)
        partial_w = lax.optimization_barrier(partial_w)
        return (accumulated + partial_w.astype(jnp.float32), None)
    accumulated, _ = lax.scan(weight_step, jnp.zeros((D, 3 * HALF_HEAD_COUNT * HD), jnp.float32), (tokens.reshape(N_SEQ, TOK_DEV, D), grad_flat.reshape(N_SEQ, TOK_DEV, 3 * HALF_HEAD_COUNT * HD)))
    grad_weights = (accumulated / jnp.sqrt(jnp.float32(SEQUENCE_TOKENS))).reshape(D, 3, HALF_HEAD_COUNT * HD).astype(jnp.bfloat16)
    return (attended, grad_tokens, grad_weights)
```

```python
import functools
import math

import jax
import jax.numpy as jnp
from jax import lax
from jax.experimental import pallas as pl
from jax.experimental.pallas import tpu as pltpu
from jax.sharding import PartitionSpec as P

HD = 128
EPSILON = 1e-06
NX, NY, NC, NZ = 4, 4, 2, 8
T, HALF = 512, 256
HEADS = 2
BLK = 128
F32, BF16 = jnp.float32, jnp.bfloat16
MESH = pl.DeviceIdType.MESH
COPIES = 99

NT = (((1,), (1,)), ((), ()))
TN = (((0,), (0,)), ((), ()))


def mm(a, b, dims=(((1,), (0,)), ((), ()))):
    return lax.dot_general(a, b, dims, preferred_element_type=F32)


def sigmoid(v):
    return 1.0 / (1.0 + jnp.exp(-v))


def kernel(
    tok_ref, w_ref, ld_ref, cot_ref, att_ref, gt_ref, gw_ref,
    tokb, wb, acc, act, grad, rc, rr, mix, mixt, sc, inside, gout, gkv, normed,
    ttc, tty, ttx, fc, fy, fx, bc, by, bx, carried,
    pbuf, sr, sl, rrv, rlv, pw, rpart, cs, rb, dsum, ra,
    ssem, rsem,
):
    z = lax.axis_index("dp")
    s = lax.axis_index("seq")
    c = lax.rem(s, 2)
    y = lax.rem(lax.div(s, 2), 4)
    x = lax.div(s, 8)
    d = 1 - c
    zr, zl = lax.rem(z + 1, NZ), lax.rem(z + NZ - 1, NZ)

    def ring(v, k):
        return lax.rem(v + k, 4)

    def place(px, py, pc):
        return (px * NY + py) * NC + pc

    partner = place(x, y, d)
    x_peer = [place(ring(x, k), y, c) for k in (1, 2, 3)]
    y_peer = [place(x, ring(y, k), c) for k in (1, 2, 3)]
    a_peer = [place(ring(x, k * d), ring(y, k * c), c) for k in (1, 2, 3)]
    b_peer = [place(ring(x, k * c), ring(y, k * d), c) for k in (1, 2, 3)]

    sent = []

    def send(src, dst, **dev):
        i = len(sent)
        copy = pltpu.make_async_remote_copy(
            src_ref=src, dst_ref=dst, send_sem=ssem.at[i], recv_sem=rsem.at[i],
            device_id=dev, device_id_type=MESH,
        )
        copy.start()
        sent.append(copy)
        return copy

    barrier = pltpu.get_barrier_semaphore()
    for peer in [partner] + x_peer + y_peer:
        pl.semaphore_signal(barrier, inc=1, device_id={"seq": peer}, device_id_type=MESH)
    for peer in (zr, zl):
        pl.semaphore_signal(barrier, inc=1, device_id={"dp": peer}, device_id_type=MESH)
    pl.semaphore_wait(barrier, 9)

    first = (0, 1)
    way = (zr, zl)
    zc = {}
    for h in (0, 1):
        for w in (0, 1):
            half = h if w == 0 else 1 - h
            zc[w, 0, half] = send(tok_ref.at[half], tokb.at[z, half], dp=way[w])
    wa = [send(w_ref, wb.at[s], seq=p) for p in a_peer]
    wp = [send(w_ref, wb.at[s], seq=partner)]
    tokb[z] = tok_ref[...]
    wb[s] = w_ref[...]

    def decay_rows(i, total):
        h, b = lax.div(i, 4), lax.rem(i, 4)
        rows = pl.ds(pl.multiple_of(b * BLK, BLK), BLK)
        row_id = b * BLK + lax.broadcasted_iota(jnp.int32, (BLK, T), 0)
        col_id = lax.broadcasted_iota(jnp.int32, (BLK, T), 1)
        run = jnp.sum(jnp.where(col_id <= row_id, ld_ref[h], 0.0), axis=1, keepdims=True)
        rc[h, rows, :] = jnp.broadcast_to(run, (BLK, BLK))
        return total

    lax.fori_loop(0, 8, decay_rows, 0)
    for h in range(HEADS):
        row = jnp.zeros((1, T), F32)
        for b in range(4):
            row_id = b * BLK + lax.broadcasted_iota(jnp.int32, (BLK, T), 0)
            col_id = lax.broadcasted_iota(jnp.int32, (BLK, T), 1)
            run = rc[h, b * BLK:(b + 1) * BLK, 0:1]
            row = row + jnp.sum(jnp.where(row_id == col_id, run, 0.0), axis=0, keepdims=True)
        rr[h] = row
        ttc[c, h] = rc[h, T - 8:T, :][7:8, :] + jnp.zeros((8, 128), F32)
    tc_copy = send(ttc.at[c], ttc.at[c], seq=partner)

    def mixing(i, zero):
        h, b = lax.div(i, 4), lax.rem(i, 4)
        rows = pl.ds(pl.multiple_of(b * BLK, BLK), BLK)
        row_id = b * BLK + lax.broadcasted_iota(jnp.int32, (BLK, T), 0)
        col_id = lax.broadcasted_iota(jnp.int32, (BLK, T), 1)
        spread = rc[h, rows, 0:1] - rr[h]
        mix[h, rows, :] = jnp.where(row_id >= col_id, jnp.exp(jnp.minimum(spread, 0.0)), 0.0)
        mixt[h, rows, :] = jnp.where(row_id <= col_id, jnp.exp(jnp.minimum(-spread, 0.0)), 0.0)
        return zero

    lax.fori_loop(0, 8, mixing, 0)
    tc_copy.wait_recv()
    tty[y] = ttc[0] + ttc[1]
    ty_copy = [send(tty.at[y], tty.at[y], seq=p) for p in y_peer]

    for copy in wa:
        copy.wait_recv()
    wbc = []
    for k in (1, 2, 3):
        for m in range(4):
            src = place(m * d + x * c, y * d + m * c, c)
            wbc.append(send(wb.at[src], wb.at[src], seq=b_peer[k - 1]))
    for k in (1, 2, 3):
        src = place(ring(x, (4 - k) * d), ring(y, (4 - k) * c), c)
        wp.append(send(wb.at[src], wb.at[src], seq=partner))

    def pass_on(k):
        for half in (0, 1):
            for w in (0, 1):
                h = half if w == 0 else 1 - half
                if k == 3 and h != first[w]:
                    continue
                zc[w, k - 1, h].wait_recv()
                shard = lax.rem(z + (NZ - k if w == 0 else k), NZ)
                zc[w, k, h] = send(tokb.at[shard, h], tokb.at[shard, h], dp=way[w])

    def hand_over(k):
        for m in range(4):
            wbc[4 * (k - 1) + m].wait_recv()
        for m in range(4):
            back = 4 - k
            src = place(m * d + ring(x, back) * c, ring(y, back) * d + m * c, c)
            wp.append(send(wb.at[src], wb.at[src], seq=partner))

    pass_on(1)
    for copy in ty_copy:
        copy.wait_recv()
    ttx[x] = tty[0] + tty[1] + tty[2] + tty[3]
    tx_copy = [send(ttx.at[x], ttx.at[x], seq=p) for p in x_peer]
    pass_on(2)
    hand_over(1)
    hand_over(3)
    for copy in tx_copy:
        copy.wait_recv()
    hand_over(2)
    pass_on(3)
    for copy in wp:
        copy.wait_recv()

    def weight_block(b):
        return wb[pl.ds(4 * b, 4)].reshape(T, 768)

    def project(b, start=False):
        part = mm(tokb[b].reshape(T, T), weight_block(b))
        if start:
            acc[...] = part
        else:
            acc[...] += part

    project(z, True)

    def project_near(i, zero):
        project(lax.rem(z + NZ - 2 + i + lax.div(i, 2), NZ))
        return zero

    lax.fori_loop(0, 4, project_near, 0)
    for w in (0, 1):
        zc[w, 2, 1 - first[w]].wait_recv()

    def project_far(i, zero):
        project(lax.rem(z + 3 + 2 * i, NZ))
        return zero

    lax.fori_loop(0, 2, project_far, 0)
    for w in (0, 1):
        zc[w, 3, first[w]].wait_recv()
    project(lax.rem(z + 4, NZ))

    def head(part, h):
        return slice(part * 256 + h * HD, part * 256 + (h + 1) * HD)

    def scalar(flag):
        return flag.astype(F32)

    zq = acc[:, 0:512]
    act[:, 0:512] = (zq * sigmoid(zq)).astype(BF16)
    act[:, 512:768] = acc[:, 512:768].astype(BF16)
    lead, fade = [], []
    for h in range(HEADS):
        keys = act[:, head(1, h)].astype(F32) * jnp.exp(ttc[c, h, 0:1, :] - rc[h])
        fc[c, h] = mm(keys.astype(BF16), act[:, head(2, h)], TN).astype(BF16)
    f_core = send(fc.at[c], fc.at[c], seq=partner)

    def tot(ref, i, h):
        return ref[i, h, 0:1, :]

    def between(ref, h, lo, hi, n=4):
        out = jnp.zeros((1, 128), F32)
        for i in range(n):
            out = out + scalar(jnp.logical_and(i > lo, i < hi)) * tot(ref, i, h)
        return out

    def wide(ref, i, h):
        return ref[i, h].astype(F32)

    def local_scores(h):
        q, k, v = (act[:, head(p, h)] for p in range(3))
        p = (mm(q, k, NT) * mix[h]).astype(BF16)
        inside[h] = mm(p, v)
        sc[h] = (mm(k, q, NT) * mixt[h]).astype(BF16)

    local_scores(0)
    f_core.wait_recv()
    for h in range(HEADS):
        fy[y, h] = (jnp.exp(tot(ttc, 1, h)) * wide(fc, 0, h) + wide(fc, 1, h)).astype(BF16)
    f_y = [send(fy.at[y], fy.at[y], seq=p) for p in y_peer]
    local_scores(1)
    for copy in f_y:
        copy.wait_recv()
    for h in range(HEADS):
        whole = jnp.zeros((HD, HD), F32)
        for i in range(4):
            whole = whole + jnp.exp(between(tty, h, i, 4)) * wide(fy, i, h)
        fx[x, h] = whole.astype(BF16)
    f_x = [send(fx.at[x], fx.at[x], seq=p) for p in x_peer]
    pre = []
    for h in range(HEADS):
        part = jnp.zeros((HD, HD), F32)
        for i in range(4):
            part = part + scalar(i < y) * jnp.exp(between(tty, h, i, y)) * wide(fy, i, h)
        carried[h] = part
    for copy in f_x:
        copy.wait_recv()
    for h in range(HEADS):
        part = jnp.zeros((HD, HD), F32)
        for i in range(4):
            part = part + scalar(i < x) * jnp.exp(between(ttx, h, i, x)) * wide(fx, i, h)
        chip = carried[h] + jnp.exp(between(tty, h, -1, y)) * part
        own = jnp.exp(scalar(c) * tot(ttc, 0, h)) * chip + scalar(c) * wide(fc, 0, h)
        carried[h] = own
        q = act[:, head(0, h)]
        leading = jnp.exp(rc[h])
        attention = inside[h] + leading * mm(q, own.astype(BF16))
        scale = jnp.sqrt(jnp.mean(attention * attention, axis=1, keepdims=True) + EPSILON)
        norm = attention / scale
        att_ref[:, h * HD:(h + 1) * HD] = norm.astype(BF16)
        up = cot_ref[:, h * HD:(h + 1) * HD].astype(F32)
        g = (up - norm * jnp.mean(up * norm, axis=1, keepdims=True)) / scale
        gout[h] = g.astype(BF16)
        ql = (q.astype(F32) * leading).astype(BF16)
        bc[c, h] = mm(ql, gout[h], TN).astype(BF16)
    b_core = send(bc.at[c], bc.at[c], seq=partner)

    def local_grads(h):
        q, k, v = (act[:, head(p, h)] for p in range(3))
        g = gout[h]
        through = (mm(g, v, NT) * mix[h]).astype(BF16)
        gq = mm(through, k) + jnp.exp(rc[h]) * mm(g, carried[h].astype(BF16), NT)
        zq = acc[:, head(0, h)]
        sg = sigmoid(zq)
        grad[:, head(0, h)] = (gq * (sg * (1.0 + zq * (1.0 - sg)))).astype(BF16)
        through = (mm(v, g, NT) * mixt[h]).astype(BF16)
        gkv[h] = mm(through, q)
        gkv[2 + h] = mm(sc[h], g)
        zk = acc[:, head(1, h)]
        sg = sigmoid(zk)
        acc[:, head(1, h)] = sg * (1.0 + zk * (1.0 - sg))

    local_grads(0)
    b_core.wait_recv()
    for h in range(HEADS):
        by[y, h] = (wide(bc, 0, h) + jnp.exp(tot(ttc, 0, h)) * wide(bc, 1, h)).astype(BF16)
    b_y = [send(by.at[y], by.at[y], seq=p) for p in y_peer]
    local_grads(1)
    for copy in b_y:
        copy.wait_recv()
    for h in range(HEADS):
        whole = jnp.zeros((HD, HD), F32)
        for i in range(4):
            whole = whole + jnp.exp(between(tty, h, -1, i)) * wide(by, i, h)
        bx[x, h] = whole.astype(BF16)
    b_x = [send(bx.at[x], bx.at[x], seq=p) for p in x_peer]
    for h in range(HEADS):
        part = jnp.zeros((HD, HD), F32)
        for i in range(4):
            part = part + scalar(i > y) * jnp.exp(between(tty, h, y, i)) * wide(by, i, h)
        carried[h] = part
    for copy in b_x:
        copy.wait_recv()
    for h in range(HEADS):
        part = jnp.zeros((HD, HD), F32)
        for i in range(4):
            part = part + scalar(i > x) * jnp.exp(between(ttx, h, x, i)) * wide(bx, i, h)
        chip = carried[h] + jnp.exp(between(tty, h, y, 4)) * part
        future = jnp.exp(scalar(d) * tot(ttc, 1, h)) * chip + scalar(d) * wide(bc, 1, h)
        future = future.astype(BF16)
        k, v = act[:, head(1, h)], act[:, head(2, h)]
        fading = jnp.exp(ttc[c, h, 0:1, :] - rc[h])
        gk = gkv[h] + fading * mm(v, future, NT)
        grad[:, head(1, h)] = (gk * acc[:, head(1, h)]).astype(BF16)
        grad[:, head(2, h)] = (gkv[2 + h] + fading * mm(k, future)).astype(BF16)

    def token_part(b):
        pbuf[b] = mm(grad[...], weight_block(b), NT).reshape(2, HALF, T)

    bufs_s, bufs_r = (sr, sl), (rrv, rlv)
    gz = {}

    def block_at(w, k):
        return lax.rem(z + (4 - k if w == 0 else 4 + k), NZ)

    def send_sum(w, k, h):
        val = pbuf[block_at(w, k), h]
        if k > 0 and (w, k - 1, h) in gz:
            gz[w, k - 1, h].wait_recv()
            val = val + bufs_r[w][k - 1, h].astype(F32)
        bufs_s[w][k, h] = val.astype(BF16)
        gz[w, k, h] = send(bufs_s[w].at[k, h], bufs_r[w].at[k, h], dp=way[w])

    token_part(lax.rem(z + 4, NZ))
    send_sum(0, 0, 0)
    send_sum(1, 0, 1)

    def parts_far(i, zero):
        token_part(lax.rem(z + 3 + 2 * i, NZ))
        return zero

    lax.fori_loop(0, 2, parts_far, 0)
    send_sum(0, 1, 1)
    send_sum(1, 1, 0)

    def weight_part(b, zero):
        part = mm(tokb[b].reshape(T, T), grad[...], TN)
        pw[pl.ds(2 * b, 2)] = part.astype(BF16).reshape(2, 2, 128, 768)
        return zero

    gp = []
    for i in range(4):
        lax.fori_loop(2 * i, 2 * i + 2, weight_part, 0)
        gp.append(
            send(pw.at[4 * i:4 * i + 4, d], rpart.at[4 * i:4 * i + 4], seq=partner)
        )
        if i == 1:
            send_sum(0, 1, 0)
            send_sum(1, 1, 1)

    def parts_near(i, zero):
        token_part(lax.rem(z + NZ - 2 + i, NZ))
        return zero

    lax.fori_loop(0, 5, parts_near, 0)

    def chip_sum(i, zero):
        cs[i] = (pw[i, c].astype(F32) + rpart[i].astype(F32)).astype(BF16)
        return zero

    send_sum(0, 2, 1)
    send_sum(1, 2, 0)
    for i in range(4):
        gp[i].wait_recv()
    lax.fori_loop(0, 16, chip_sum, 0)
    gb = []
    for k in (1, 2, 3):
        for m in range(4):
            src = (m * d + ring(x, k) * c) * NY + ring(y, k) * d + m * c
            gb.append(send(cs.at[src], rb.at[k - 1, m], seq=b_peer[k - 1]))
    send_sum(0, 2, 0)
    send_sum(1, 2, 1)
    send_sum(0, 3, 1)
    send_sum(1, 3, 0)
    send_sum(0, 3, 0)
    send_sum(1, 3, 1)
    for copy in gb:
        copy.wait_recv()
    for m in range(4):
        own = (m * d + x * c) * NY + y * d + m * c
        val = cs[own].astype(F32)
        for k in range(3):
            val = val + rb[k, m].astype(F32)
        dsum[m] = val.astype(BF16)
    at = x * d + y * c
    ga = [send(dsum.at[ring(at, k)], ra.at[k - 1], seq=a_peer[k - 1]) for k in (1, 2, 3)]
    for copy in ga:
        copy.wait_recv()
    val = dsum[at].astype(F32)
    for k in range(3):
        val = val + ra[k].astype(F32)
    gw_ref[...] = (val * (1.0 / math.sqrt(16384.0))).astype(BF16)
    for h in (1, 0):
        gz[0, 3, h].wait_recv()
        gz[1, 3, h].wait_recv()
        val = pbuf[z, h] + rrv[3, h].astype(F32) + rlv[3, h].astype(F32)
        gt_ref[h] = val.astype(BF16)
    for copy in sent:
        copy.wait_send()
    assert len(sent) == COPIES, len(sent)


def local(tokens, weights, log_decay, cotangent):
    vmem = pl.BlockSpec(memory_space=pltpu.VMEM)
    V = pltpu.VMEM
    state = (2, HEADS, HD, HD)
    states = (4, HEADS, HD, HD)
    scratch = [
        V((NZ, 2, HALF, T), BF16),
        V((32, 128, 768), BF16),
        V((T, 768), F32),
        V((T, 768), BF16),
        V((T, 768), BF16),
        V((HEADS, T, 128), F32),
        V((HEADS, 1, T), F32),
        V((HEADS, T, T), F32),
        V((HEADS, T, T), F32),
        V((HEADS, T, T), BF16),
        V((HEADS, T, HD), F32),
        V((HEADS, T, HD), BF16),
        V((4, T, HD), F32),
        V((8, 128), F32),
        V((2, HEADS, 8, 128), F32),
        V((4, HEADS, 8, 128), F32),
        V((4, HEADS, 8, 128), F32),
        V(state, BF16), V(states, BF16), V(states, BF16),
        V(state, BF16), V(states, BF16), V(states, BF16),
        V((HEADS, HD, HD), F32),
        V((NZ, 2, HALF, T), F32),
        V((4, 2, HALF, T), BF16), V((4, 2, HALF, T), BF16),
        V((4, 2, HALF, T), BF16), V((4, 2, HALF, T), BF16),
        V((16, 2, 128, 768), BF16),
        V((16, 128, 768), BF16),
        V((16, 128, 768), BF16),
        V((3, 4, 128, 768), BF16),
        V((4, 128, 768), BF16),
        V((3, 128, 768), BF16),
        pltpu.SemaphoreType.DMA((COPIES,)),
        pltpu.SemaphoreType.DMA((COPIES,)),
    ]
    attended, grad_tokens, grad_weights = pl.pallas_call(
        kernel,
        out_shape=(
            jax.ShapeDtypeStruct((T, 256), BF16),
            jax.ShapeDtypeStruct((2, HALF, T), BF16),
            jax.ShapeDtypeStruct((128, 768), BF16),
        ),
        in_specs=[vmem] * 4,
        out_specs=(vmem,) * 3,
        scratch_shapes=scratch,
        compiler_params=pltpu.CompilerParams(
            collective_id=0, has_side_effects=True, vmem_limit_bytes=60 << 20
        ),
        name="layer",
    )(
        tokens.reshape(2, HALF, T),
        weights.reshape(128, 768),
        log_decay.reshape(HEADS, 1, T),
        cotangent,
    )
    return attended, grad_tokens.reshape(T, T), grad_weights.reshape(128, 3, 256)


def solution(mesh):
    return jax.shard_map(
        local,
        mesh=mesh,
        in_specs=(P("seq", "dp"), P("seq", None, "dp"), P("dp", "seq"), P("seq", "dp")),
        out_specs=(P("seq", "dp"), P("seq", "dp"), P("seq", None, "dp")),
        check_vma=False,
    )
```

```python
import functools
import math

import jax
import jax.numpy as jnp
from jax import lax
from jax.experimental import pallas as pl
from jax.experimental.pallas import tpu as pltpu
from jax.sharding import PartitionSpec as P

HD = 128
EPSILON = 1e-06
NX, NY, NC, NZ = 4, 4, 2, 8
T, HALF = 512, 256
HEADS = 2
BLK = 128
F32, BF16 = jnp.float32, jnp.bfloat16
MESH = pl.DeviceIdType.MESH
COPIES = 101

NT = (((1,), (1,)), ((), ()))
TN = (((0,), (0,)), ((), ()))


def mm(a, b, dims=(((1,), (0,)), ((), ()))):
    return lax.dot_general(a, b, dims, preferred_element_type=F32)


def sigmoid(v):
    return 1.0 / (1.0 + jnp.exp(-v))


def kernel(
    tok_ref, w_ref, ld_ref, cot_ref, att_ref, gt_ref, gw_ref,
    tokb, wb, cotv, attv, gtv, gwv, acc, act, grad, rc, rr, lead, fade, mix, mixt, sc,
    inside, qlt, gout, gkv, ttc, tca, wtf, wtb,
    fs, fo, fa, fm, fr, fe, fin, bs, bo, ba, bm, br, be, bin_,
    pbuf, sr, sl, rrv, rlv, pw, rpart, cs, rb, dsum, ra,
    ssem, rsem, lsem,
):
    z = lax.axis_index("dp")
    s = lax.axis_index("seq")
    c = lax.rem(s, 2)
    y = lax.rem(lax.div(s, 2), 4)
    x = lax.div(s, 8)
    d = 1 - c
    zr, zl = lax.rem(z + 1, NZ), lax.rem(z + NZ - 1, NZ)

    def ring(v, k):
        return lax.rem(v + k, 4)

    def place(px, py, pc):
        return (px * NY + py) * NC + pc

    partner = place(x, y, d)
    x_peer = [place(ring(x, k), y, c) for k in (1, 2, 3)]
    y_peer = [place(x, ring(y, k), c) for k in (1, 2, 3)]
    a_peer = [place(ring(x, k * d), ring(y, k * c), c) for k in (1, 2, 3)]
    b_peer = [place(ring(x, k * c), ring(y, k * d), c) for k in (1, 2, 3)]

    here = [
        pltpu.make_async_copy(
            w_ref.at[p], wb.at[s, :, pl.ds(256 * p, 256)], lsem.at[p]
        )
        for p in range(3)
    ]
    here.append(pltpu.make_async_copy(tok_ref, tokb.at[z], lsem.at[3]))
    here.append(pltpu.make_async_copy(cot_ref, cotv, lsem.at[4]))
    for copy in here:
        copy.start()

    sent = []

    def send(src, dst, **dev):
        i = len(sent)
        copy = pltpu.make_async_remote_copy(
            src_ref=src, dst_ref=dst, send_sem=ssem.at[i], recv_sem=rsem.at[i],
            device_id=dev, device_id_type=MESH,
        )
        copy.start()
        sent.append(copy)
        return copy

    barrier = pltpu.get_barrier_semaphore()
    for peer in [partner] + x_peer + y_peer:
        pl.semaphore_signal(barrier, inc=1, device_id={"seq": peer}, device_id_type=MESH)
    for peer in (zr, zl):
        pl.semaphore_signal(barrier, inc=1, device_id={"dp": peer}, device_id_type=MESH)
    pl.semaphore_wait(barrier, 9)

    first = (0, 1)
    way = (zr, zl)
    zc = {}
    for h in (0, 1):
        for w in (0, 1):
            half = h if w == 0 else 1 - h
            zc[w, 0, half] = send(tok_ref.at[half], tokb.at[z, half], dp=way[w])
    for copy in here[:3]:
        copy.wait()
    wa = [send(wb.at[s], wb.at[s], seq=p) for p in a_peer]
    wp = [send(wb.at[s], wb.at[s], seq=partner)]

    def decay_rows(i, total):
        h, b = lax.div(i, 4), lax.rem(i, 4)
        rows = pl.ds(pl.multiple_of(b * BLK, BLK), BLK)
        row_id = b * BLK + lax.broadcasted_iota(jnp.int32, (BLK, T), 0)
        col_id = lax.broadcasted_iota(jnp.int32, (BLK, T), 1)
        run = jnp.sum(jnp.where(col_id <= row_id, ld_ref[pl.ds(h, 1), :], 0.0), axis=1, keepdims=True)
        rc[h, rows, :] = jnp.broadcast_to(run, (BLK, BLK))
        return total

    lax.fori_loop(0, 8, decay_rows, 0)
    for h in range(HEADS):
        row = jnp.zeros((1, T), F32)
        for b in range(4):
            row_id = b * BLK + lax.broadcasted_iota(jnp.int32, (BLK, T), 0)
            col_id = lax.broadcasted_iota(jnp.int32, (BLK, T), 1)
            run = rc[h, b * BLK:(b + 1) * BLK, 0:1]
            row = row + jnp.sum(jnp.where(row_id == col_id, run, 0.0), axis=0, keepdims=True)
        rr[h] = row
        ttc[c, h] = rc[h, T - 8:T, :][7:8, :] + jnp.zeros((8, 128), F32)
    tc_copy = send(ttc.at[c], ttc.at[c], seq=partner)

    def mixing(i, zero):
        h, b = lax.div(i, 4), lax.rem(i, 4)
        rows = pl.ds(pl.multiple_of(b * BLK, BLK), BLK)
        row_id = b * BLK + lax.broadcasted_iota(jnp.int32, (BLK, T), 0)
        col_id = lax.broadcasted_iota(jnp.int32, (BLK, T), 1)
        spread = rc[h, rows, 0:1] - rr[h]
        mix[h, rows, :] = jnp.where(row_id >= col_id, jnp.exp(jnp.minimum(spread, 0.0)), 0.0)
        mixt[h, rows, :] = jnp.where(row_id <= col_id, jnp.exp(jnp.minimum(-spread, 0.0)), 0.0)
        lead[h, rows, :] = jnp.exp(rc[h, rows, :])
        fade[h, rows, :] = jnp.exp(ttc[c, h, 0:1, :] - rc[h, rows, :])
        return zero

    lax.fori_loop(0, 8, mixing, 0)
    tc_copy.wait_recv()
    chip = x * NY + y
    tca[chip] = ttc[0] + ttc[1]
    ty_copy = [send(tca.at[chip], tca.at[chip], seq=p) for p in y_peer]

    for copy in wa:
        copy.wait_recv()
    wbc = []
    for k in (1, 2, 3):
        for m in range(4):
            src = place(m * d + x * c, y * d + m * c, c)
            wbc.append(send(wb.at[src], wb.at[src], seq=b_peer[k - 1]))
    for k in (1, 2, 3):
        src = place(ring(x, (4 - k) * d), ring(y, (4 - k) * c), c)
        wp.append(send(wb.at[src], wb.at[src], seq=partner))

    def pass_on(k):
        for half in (0, 1):
            for w in (0, 1):
                h = half if w == 0 else 1 - half
                if k == 3 and h != first[w]:
                    continue
                zc[w, k - 1, h].wait_recv()
                shard = lax.rem(z + (NZ - k if w == 0 else k), NZ)
                zc[w, k, h] = send(tokb.at[shard, h], tokb.at[shard, h], dp=way[w])

    def hand_over(k):
        for m in range(4):
            wbc[4 * (k - 1) + m].wait_recv()
        for m in range(4):
            back = 4 - k
            src = place(m * d + ring(x, back) * c, ring(y, back) * d + m * c, c)
            wp.append(send(wb.at[src], wb.at[src], seq=partner))

    pass_on(1)
    for copy in ty_copy:
        copy.wait_recv()
    line = pl.ds(NY * x, NY)
    tx_copy = [send(tca.at[line], tca.at[line], seq=p) for p in x_peer]
    pass_on(2)
    hand_over(1)
    hand_over(3)
    for copy in tx_copy:
        copy.wait_recv()
    hand_over(2)
    pass_on(3)

    def weigh(n, zero):
        k, i = lax.div(n, 4), lax.rem(n, 4)
        p = (x * d + i * c) * NY + i * d + y * c
        q = ring(x, k * d) * NY + ring(y, k * c)
        ahead = jnp.zeros((8, 128), F32)
        behind = jnp.zeros((8, 128), F32)
        for j in range(NX * NY):
            total = tca[j, c]
            ahead = ahead + jnp.logical_and(j > p, j < q).astype(F32) * total
            behind = behind + jnp.logical_and(j < p, j > q).astype(F32) * total
        wtf[n] = (p < q).astype(F32) * jnp.exp(ahead)
        wtb[n] = (p > q).astype(F32) * jnp.exp(behind)
        return zero

    lax.fori_loop(0, 16, weigh, 0)
    here[3].wait()
    here[4].wait()
    for copy in wp:
        copy.wait_recv()

    def weight_block(b):
        return wb[pl.ds(4 * b, 4)].reshape(T, 768)

    def project(b, start=False):
        part = mm(tokb[b].reshape(T, T), weight_block(b))
        if start:
            acc[...] = part
        else:
            acc[...] += part

    project(z, True)

    def project_near(i, zero):
        project(lax.rem(z + NZ - 2 + i + lax.div(i, 2), NZ))
        return zero

    lax.fori_loop(0, 4, project_near, 0)
    for w in (0, 1):
        zc[w, 2, 1 - first[w]].wait_recv()

    def project_far(i, zero):
        project(lax.rem(z + 3 + 2 * i, NZ))
        return zero

    lax.fori_loop(0, 2, project_far, 0)
    for w in (0, 1):
        zc[w, 3, first[w]].wait_recv()
    project(lax.rem(z + 4, NZ))

    def head(part, h):
        return slice(part * 256 + h * HD, part * 256 + (h + 1) * HD)

    def scalar(flag):
        return flag.astype(F32)

    t0, t1 = ttc[0, c, 0:1, :], ttc[1, c, 0:1, :]
    fc, fd = scalar(c), scalar(d)

    def mine(ref, j=None):
        return (ref[...] if j is None else ref[j]).astype(F32)

    def exchange(own, other, line, out, into, leave, entry, weights, wo, wp, we, ke, wi, ki, fill):
        swap = send(own.at[d], other, seq=partner)
        fill[0]()
        swap.wait_recv()
        at = y * d + x * c
        line[at] = (wo * mine(own, c) + wp * mine(other)).astype(BF16)
        stage = [send(line.at[at], line.at[at], seq=p) for p in b_peer]
        fill[1]()
        for copy in stage:
            copy.wait_recv()

        def message(k):
            val = weights[4 * k, 0:1, :] * mine(line, 0)
            for i in (1, 2, 3):
                val = val + weights[4 * k + i, 0:1, :] * mine(line, i)
            return val

        stage = []
        for k in (2, 1, 3):
            out[k] = message(k).astype(BF16)
            stage.append(send(out.at[k], into.at[k], seq=a_peer[k - 1]))
        total = message(0)
        fill[2]()
        for copy in stage:
            copy.wait_recv()
        for k in (1, 2, 3):
            total = total + mine(into, k)
        leave[...] = (we * total + ke * mine(own, c)).astype(BF16)
        swap = send(leave, entry.at[c], seq=partner)
        entry[c] = (wi * total + ki * mine(other)).astype(BF16)
        swap.wait_recv()

    act[:, 512:768] = acc[:, 512:768].astype(BF16)
    zk = acc[:, 256:512]
    act[:, 256:512] = (zk * sigmoid(zk)).astype(BF16)
    for h in range(HEADS):
        keys = act[:, head(1, h)].astype(F32) * fade[h]
        fs[h] = mm(keys.astype(BF16), act[:, head(2, h)], TN).astype(BF16)

    def queries():
        zq = acc[:, 0:256]
        act[:, 0:256] = (zq * sigmoid(zq)).astype(BF16)

    def local_scores(h):
        q, k, v = (act[:, head(p, h)] for p in range(3))
        p = (mm(q, k, NT) * mix[h]).astype(BF16)
        inside[h] = mm(p, v)
        sc[h] = (mm(k, q, NT) * mixt[h]).astype(BF16)
        qlt[h] = (q.astype(F32) * lead[h]).T.astype(BF16)

    exchange(
        fs, fo, fa, fm, fr, fe, fin, wtf,
        jnp.exp(fd * t1), jnp.exp(fc * t1), jnp.exp(fd * t0), fd, jnp.exp(fc * t0), fc,
        (queries, lambda: local_scores(0), lambda: local_scores(1)),
    )
    for h in range(HEADS):
        q = act[:, head(0, h)]
        attention = inside[h] + lead[h] * mm(q, fin[h])
        scale = jnp.sqrt(jnp.mean(attention * attention, axis=1, keepdims=True) + EPSILON)
        norm = attention / scale
        attv[:, h * HD:(h + 1) * HD] = norm.astype(BF16)
        up = cotv[:, h * HD:(h + 1) * HD].astype(F32)
        g = (up - norm * jnp.mean(up * norm, axis=1, keepdims=True)) / scale
        gout[h] = g.astype(BF16)
        bs[h] = mm(qlt[h], gout[h]).astype(BF16)
    leaving = [pltpu.make_async_copy(attv, att_ref, lsem.at[5])]
    leaving[0].start()

    def local_grads(h):
        q, k, v = (act[:, head(p, h)] for p in range(3))
        g = gout[h]
        through = (mm(g, v, NT) * mix[h]).astype(BF16)
        gq = mm(through, k) + lead[h] * mm(g, fin[h], NT)
        zq = acc[:, head(0, h)]
        sg = sigmoid(zq)
        grad[:, head(0, h)] = (gq * (sg * (1.0 + zq * (1.0 - sg)))).astype(BF16)
        through = (mm(v, g, NT) * mixt[h]).astype(BF16)
        gkv[h] = mm(through, q)
        gkv[2 + h] = mm(sc[h], g)
        zk = acc[:, head(1, h)]
        sg = sigmoid(zk)
        acc[:, head(1, h)] = sg * (1.0 + zk * (1.0 - sg))

    exchange(
        bs, bo, ba, bm, br, be, bin_, wtb,
        jnp.exp(fc * t0), jnp.exp(fd * t0), jnp.exp(fc * t1), fc, jnp.exp(fd * t1), fd,
        (lambda: None, lambda: local_grads(0), lambda: local_grads(1)),
    )
    for h in range(HEADS):
        future = bin_[h]
        k, v = act[:, head(1, h)], act[:, head(2, h)]
        gk = gkv[h] + fade[h] * mm(v, future, NT)
        grad[:, head(1, h)] = (gk * acc[:, head(1, h)]).astype(BF16)
        grad[:, head(2, h)] = (gkv[2 + h] + fade[h] * mm(k, future)).astype(BF16)

    def token_part(b):
        pbuf[b] = mm(grad[...], weight_block(b), NT).reshape(2, HALF, T)

    bufs_s, bufs_r = (sr, sl), (rrv, rlv)
    gz = {}

    def block_at(w, k):
        return lax.rem(z + (4 - k if w == 0 else 4 + k), NZ)

    def send_sum(w, k, h):
        val = pbuf[block_at(w, k), h]
        if k > 0 and (w, k - 1, h) in gz:
            gz[w, k - 1, h].wait_recv()
            val = val + bufs_r[w][k - 1, h].astype(F32)
        bufs_s[w][k, h] = val.astype(BF16)
        gz[w, k, h] = send(bufs_s[w].at[k, h], bufs_r[w].at[k, h], dp=way[w])

    far = lax.rem(z + 4, NZ)
    for h in (0, 1):
        rows = slice(h * HALF, (h + 1) * HALF)
        pbuf[far, h] = mm(grad[rows, :], weight_block(far), NT)
        send_sum(h, 0, h)

    def parts_far(i, zero):
        token_part(lax.rem(z + 3 + 2 * i, NZ))
        return zero

    lax.fori_loop(0, 2, parts_far, 0)
    send_sum(0, 1, 1)
    send_sum(1, 1, 0)

    def weight_part(b, zero):
        part = mm(tokb[b].reshape(T, T), grad[...], TN)
        pw[pl.ds(2 * b, 2)] = part.astype(BF16).reshape(2, 2, 128, 768)
        return zero

    gp = []
    for i in range(4):
        lax.fori_loop(2 * i, 2 * i + 2, weight_part, 0)
        gp.append(
            send(pw.at[4 * i:4 * i + 4, d], rpart.at[4 * i:4 * i + 4], seq=partner)
        )
        if i == 1:
            send_sum(0, 1, 0)
            send_sum(1, 1, 1)

    def parts_near(i, zero):
        token_part(lax.rem(z + NZ - 2 + i, NZ))
        return zero

    lax.fori_loop(0, 5, parts_near, 0)

    def chip_sum(i, zero):
        cs[i] = (pw[i, c].astype(F32) + rpart[i].astype(F32)).astype(BF16)
        return zero

    send_sum(0, 2, 1)
    send_sum(1, 2, 0)
    for i in range(4):
        gp[i].wait_recv()
    lax.fori_loop(0, 16, chip_sum, 0)
    gb = []
    for k in (1, 2, 3):
        for m in range(4):
            src = (m * d + ring(x, k) * c) * NY + ring(y, k) * d + m * c
            gb.append(send(cs.at[src], rb.at[k - 1, m], seq=b_peer[k - 1]))
    send_sum(0, 2, 0)
    send_sum(1, 2, 1)
    send_sum(0, 3, 1)
    send_sum(1, 3, 0)
    send_sum(0, 3, 0)
    send_sum(1, 3, 1)
    for copy in gb:
        copy.wait_recv()
    for m in range(4):
        own = (m * d + x * c) * NY + y * d + m * c
        val = cs[own].astype(F32)
        for k in range(3):
            val = val + rb[k, m].astype(F32)
        dsum[m] = val.astype(BF16)
    at = x * d + y * c
    ga = [send(dsum.at[ring(at, k)], ra.at[k - 1], seq=a_peer[k - 1]) for k in (1, 2, 3)]
    for copy in ga:
        copy.wait_recv()
    val = dsum[at].astype(F32)
    for k in range(3):
        val = val + ra[k].astype(F32)
    gwv[...] = (val * (1.0 / math.sqrt(16384.0))).astype(BF16)
    for p in range(3):
        leaving.append(
            pltpu.make_async_copy(gwv.at[:, pl.ds(256 * p, 256)], gw_ref.at[p], lsem.at[6 + p])
        )
        leaving[-1].start()
    for h in (1, 0):
        gz[0, 3, h].wait_recv()
        gz[1, 3, h].wait_recv()
        val = pbuf[z, h] + rrv[3, h].astype(F32) + rlv[3, h].astype(F32)
        gtv[h] = val.astype(BF16)
        leaving.append(pltpu.make_async_copy(gtv.at[h], gt_ref.at[h], lsem.at[9 + h]))
        leaving[-1].start()
    for copy in leaving:
        copy.wait()
    for copy in sent:
        copy.wait_send()
    assert len(sent) == COPIES, len(sent)


def local(tokens, weights, log_decay, cotangent):
    vmem = pl.BlockSpec(memory_space=pltpu.VMEM)
    hbm = pl.BlockSpec(memory_space=pl.ANY)
    V = pltpu.VMEM
    states = [
        V((HEADS, HD, HD), BF16),
        V((HD, HD), BF16),
        V((4, HD, HD), BF16),
        V((4, HD, HD), BF16), V((4, HD, HD), BF16),
        V((HD, HD), BF16),
        V((HEADS, HD, HD), BF16),
    ]
    scratch = [
        V((NZ, 2, HALF, T), BF16),
        V((32, 128, 768), BF16),
        V((T, 256), BF16), V((T, 256), BF16),
        V((2, HALF, T), BF16), V((128, 768), BF16),
        V((T, 768), F32),
        V((T, 768), BF16),
        V((T, 768), BF16),
        V((HEADS, T, 128), F32),
        V((HEADS, 1, T), F32),
        V((HEADS, T, 128), F32), V((HEADS, T, 128), F32),
        V((HEADS, T, T), F32),
        V((HEADS, T, T), F32),
        V((HEADS, T, T), BF16),
        V((HEADS, T, HD), F32),
        V((HEADS, HD, T), BF16),
        V((HEADS, T, HD), BF16),
        V((4, T, HD), F32),
        V((2, HEADS, 8, 128), F32),
        V((16, HEADS, 8, 128), F32),
        V((16, 8, 128), F32), V((16, 8, 128), F32),
    ] + states + states + [
        V((NZ, 2, HALF, T), F32),
        V((4, 2, HALF, T), BF16), V((4, 2, HALF, T), BF16),
        V((4, 2, HALF, T), BF16), V((4, 2, HALF, T), BF16),
        V((16, 2, 128, 768), BF16),
        V((16, 128, 768), BF16),
        V((16, 128, 768), BF16),
        V((3, 4, 128, 768), BF16),
        V((4, 128, 768), BF16),
        V((3, 128, 768), BF16),
        pltpu.SemaphoreType.DMA((COPIES,)),
        pltpu.SemaphoreType.DMA((COPIES,)),
        pltpu.SemaphoreType.DMA((11,)),
    ]
    attended, grad_tokens, grad_weights = pl.pallas_call(
        kernel,
        out_shape=(
            jax.ShapeDtypeStruct((T, 256), BF16),
            jax.ShapeDtypeStruct((2, HALF, T), BF16),
            jax.ShapeDtypeStruct((3, 128, 256), BF16),
        ),
        in_specs=[hbm, hbm, vmem, hbm],
        out_specs=(hbm,) * 3,
        scratch_shapes=scratch,
        compiler_params=pltpu.CompilerParams(
            collective_id=0, has_side_effects=True, vmem_limit_bytes=60 << 20
        ),
        name="layer",
    )(tokens.reshape(2, HALF, T), weights.transpose(1, 0, 2), log_decay, cotangent)
    return attended, grad_tokens.reshape(T, T), grad_weights.transpose(1, 0, 2)


def solution(mesh):
    return jax.shard_map(
        local,
        mesh=mesh,
        in_specs=(P("seq", "dp"), P("seq", None, "dp"), P("dp", "seq"), P("seq", "dp")),
        out_specs=(P("seq", "dp"), P("seq", "dp"), P("seq", None, "dp")),
        check_vma=False,
    )
```

```python
import functools
import math

import jax
import jax.numpy as jnp
from jax import lax
from jax.experimental import pallas as pl
from jax.experimental.pallas import tpu as pltpu
from jax.sharding import PartitionSpec as P

HD = 128
EPSILON = 1e-06
NX, NY, NC, NZ = 4, 4, 2, 8
T, HALF = 512, 256
HEADS = 2
BLK = 128
F32, BF16 = jnp.float32, jnp.bfloat16
MESH = pl.DeviceIdType.MESH
COPIES = 101
VMEM_LIMIT = 59800000

NT = (((1,), (1,)), ((), ()))
TN = (((0,), (0,)), ((), ()))


def mm(a, b, dims=(((1,), (0,)), ((), ()))):
    return lax.dot_general(a, b, dims, preferred_element_type=F32)


def sigmoid(v):
    return 1.0 / (1.0 + jnp.exp(-v))


def kernel(
    tok_ref, w_ref, ld_ref, cot_ref, att_ref, gt_ref, gw_ref,
    tokb, wb, cotv, ldv, acc, act, grad, rc, rr, lead, fade, mix, mixt, sc,
    inside, qlt, gout, gkv, ttc, tca, wtf, wtb,
    fs, fo, fa, fm, fr, fe, fin, bs, bo, ba, bm, br, be, bin_,
    pbuf, sr, sl, rrv, rlv, pw, rpart, cs, rb, dsum, ra,
    ssem, rsem, lsem,
):
    z = lax.axis_index("dp")
    s = lax.axis_index("seq")
    c = lax.rem(s, 2)
    y = lax.rem(lax.div(s, 2), 4)
    x = lax.div(s, 8)
    d = 1 - c
    zr, zl = lax.rem(z + 1, NZ), lax.rem(z + NZ - 1, NZ)

    def ring(v, k):
        return lax.rem(v + k, 4)

    def place(px, py, pc):
        return (px * NY + py) * NC + pc

    partner = place(x, y, d)
    x_peer = [place(ring(x, k), y, c) for k in (1, 2, 3)]
    y_peer = [place(x, ring(y, k), c) for k in (1, 2, 3)]
    a_peer = [place(ring(x, k * d), ring(y, k * c), c) for k in (1, 2, 3)]
    b_peer = [place(ring(x, k * c), ring(y, k * d), c) for k in (1, 2, 3)]

    here = [
        pltpu.make_async_copy(
            w_ref.at[p], wb.at[s, :, pl.ds(256 * p, 256)], lsem.at[p]
        )
        for p in range(3)
    ]
    here.append(pltpu.make_async_copy(tok_ref, tokb.at[z], lsem.at[3]))
    here.append(pltpu.make_async_copy(cot_ref, cotv, lsem.at[4]))
    here.append(pltpu.make_async_copy(ld_ref, ldv, lsem.at[5]))

    sent = []

    def send(src, dst, **dev):
        i = len(sent)
        copy = pltpu.make_async_remote_copy(
            src_ref=src, dst_ref=dst, send_sem=ssem.at[i], recv_sem=rsem.at[i],
            device_id=dev, device_id_type=MESH,
        )
        copy.start()
        sent.append(copy)
        return copy

    barrier = pltpu.get_barrier_semaphore()
    for peer in [partner] + x_peer + y_peer:
        pl.semaphore_signal(barrier, inc=1, device_id={"seq": peer}, device_id_type=MESH)
    for peer in (zr, zl):
        pl.semaphore_signal(barrier, inc=1, device_id={"dp": peer}, device_id_type=MESH)
    for copy in here:
        copy.start()
    pl.semaphore_wait(barrier, 9)

    first = (0, 1)
    way = (zr, zl)
    zc = {}
    for h in (0, 1):
        for w in (0, 1):
            half = h if w == 0 else 1 - h
            zc[w, 0, half] = send(tok_ref.at[half], tokb.at[z, half], dp=way[w])
    for copy in here[:3]:
        copy.wait()
    wa = [send(wb.at[s], wb.at[s], seq=p) for p in a_peer]
    wp = [send(wb.at[s], wb.at[s], seq=partner)]

    here[5].wait()
    def decay_rows(i, total):
        h, b = lax.div(i, 4), lax.rem(i, 4)
        rows = pl.ds(pl.multiple_of(b * BLK, BLK), BLK)
        row_id = b * BLK + lax.broadcasted_iota(jnp.int32, (BLK, T), 0)
        col_id = lax.broadcasted_iota(jnp.int32, (BLK, T), 1)
        run = jnp.sum(jnp.where(col_id <= row_id, ldv[pl.ds(h, 1), :], 0.0), axis=1, keepdims=True)
        rc[h, rows, :] = jnp.broadcast_to(run, (BLK, BLK))
        return total

    lax.fori_loop(0, 8, decay_rows, 0)
    for h in range(HEADS):
        row = jnp.zeros((1, T), F32)
        for b in range(4):
            row_id = b * BLK + lax.broadcasted_iota(jnp.int32, (BLK, T), 0)
            col_id = lax.broadcasted_iota(jnp.int32, (BLK, T), 1)
            run = rc[h, b * BLK:(b + 1) * BLK, 0:1]
            row = row + jnp.sum(jnp.where(row_id == col_id, run, 0.0), axis=0, keepdims=True)
        rr[h] = row
        ttc[c, h] = rc[h, T - 8:T, :][7:8, :] + jnp.zeros((8, 128), F32)
    tc_copy = send(ttc.at[c], ttc.at[c], seq=partner)

    def mixing(i, zero):
        h, b = lax.div(i, 4), lax.rem(i, 4)
        rows = pl.ds(pl.multiple_of(b * BLK, BLK), BLK)
        row_id = b * BLK + lax.broadcasted_iota(jnp.int32, (BLK, T), 0)
        col_id = lax.broadcasted_iota(jnp.int32, (BLK, T), 1)
        spread = rc[h, rows, 0:1] - rr[h]
        mix[h, rows, :] = jnp.where(row_id >= col_id, jnp.exp(jnp.minimum(spread, 0.0)), 0.0)
        mixt[h, rows, :] = jnp.where(row_id <= col_id, jnp.exp(jnp.minimum(-spread, 0.0)), 0.0)
        lead[h, rows, :] = jnp.exp(rc[h, rows, :])
        fade[h, rows, :] = jnp.exp(ttc[c, h, 0:1, :] - rc[h, rows, :])
        return zero

    lax.fori_loop(0, 8, mixing, 0)
    tc_copy.wait_recv()
    chip = x * NY + y
    tca[chip] = ttc[0] + ttc[1]
    ty_copy = [send(tca.at[chip], tca.at[chip], seq=p) for p in y_peer]

    for copy in wa:
        copy.wait_recv()
    wbc = []
    for k in (1, 2, 3):
        for m in range(4):
            src = place(m * d + x * c, y * d + m * c, c)
            wbc.append(send(wb.at[src], wb.at[src], seq=b_peer[k - 1]))
    for k in (1, 2, 3):
        src = place(ring(x, (4 - k) * d), ring(y, (4 - k) * c), c)
        wp.append(send(wb.at[src], wb.at[src], seq=partner))

    def pass_on(k):
        for half in (0, 1):
            for w in (0, 1):
                h = half if w == 0 else 1 - half
                if k == 3 and h != first[w]:
                    continue
                zc[w, k - 1, h].wait_recv()
                shard = lax.rem(z + (NZ - k if w == 0 else k), NZ)
                zc[w, k, h] = send(tokb.at[shard, h], tokb.at[shard, h], dp=way[w])

    def hand_over(k):
        for m in range(4):
            wbc[4 * (k - 1) + m].wait_recv()
        for m in range(4):
            back = 4 - k
            src = place(m * d + ring(x, back) * c, ring(y, back) * d + m * c, c)
            wp.append(send(wb.at[src], wb.at[src], seq=partner))

    pass_on(1)
    for copy in ty_copy:
        copy.wait_recv()
    line = pl.ds(NY * x, NY)
    tx_copy = [send(tca.at[line], tca.at[line], seq=p) for p in x_peer]
    pass_on(2)
    hand_over(1)
    hand_over(3)
    for copy in tx_copy:
        copy.wait_recv()
    hand_over(2)
    pass_on(3)

    def weigh(n, zero):
        k, i = lax.div(n, 4), lax.rem(n, 4)
        p = (x * d + i * c) * NY + i * d + y * c
        q = ring(x, k * d) * NY + ring(y, k * c)
        ahead = jnp.zeros((8, 128), F32)
        behind = jnp.zeros((8, 128), F32)
        for j in range(NX * NY):
            total = tca[j, c]
            ahead = ahead + jnp.logical_and(j > p, j < q).astype(F32) * total
            behind = behind + jnp.logical_and(j < p, j > q).astype(F32) * total
        wtf[n] = (p < q).astype(F32) * jnp.exp(ahead)
        wtb[n] = (p > q).astype(F32) * jnp.exp(behind)
        return zero

    lax.fori_loop(0, 16, weigh, 0)
    here[3].wait()
    here[4].wait()
    for copy in wp:
        copy.wait_recv()

    def weight_block(b):
        return wb[pl.ds(4 * b, 4)].reshape(T, 768)

    def project(b, start=False):
        part = mm(tokb[b].reshape(T, T), weight_block(b))
        if start:
            acc[...] = part
        else:
            acc[...] += part

    project(z, True)

    def project_near(i, zero):
        project(lax.rem(z + NZ - 2 + i + lax.div(i, 2), NZ))
        return zero

    lax.fori_loop(0, 4, project_near, 0)
    for w in (0, 1):
        zc[w, 2, 1 - first[w]].wait_recv()

    def project_far(i, zero):
        project(lax.rem(z + 3 + 2 * i, NZ))
        return zero

    lax.fori_loop(0, 2, project_far, 0)
    for w in (0, 1):
        zc[w, 3, first[w]].wait_recv()
    project(lax.rem(z + 4, NZ))

    def head(part, h):
        return slice(part * 256 + h * HD, part * 256 + (h + 1) * HD)

    def scalar(flag):
        return flag.astype(F32)

    t0, t1 = ttc[0, c, 0:1, :], ttc[1, c, 0:1, :]
    fc, fd = scalar(c), scalar(d)

    def mine(ref, j=None):
        return (ref[...] if j is None else ref[j]).astype(F32)

    def exchange(own, other, line, out, into, leave, entry, weights, wo, wp, we, ke, wi, ki, fill):
        swap = send(own.at[d], other, seq=partner)
        fill[0]()
        swap.wait_recv()
        at = y * d + x * c
        line[at] = (wo * mine(own, c) + wp * mine(other)).astype(BF16)
        stage = [send(line.at[at], line.at[at], seq=b_peer[k]) for k in (1, 0, 2)]
        fill[1]()
        for copy in stage:
            copy.wait_recv()

        def message(k):
            val = weights[4 * k, 0:1, :] * mine(line, 0)
            for i in (1, 2, 3):
                val = val + weights[4 * k + i, 0:1, :] * mine(line, i)
            return val

        stage = []
        for k in (2, 1, 3):
            out[k] = message(k).astype(BF16)
            stage.append(send(out.at[k], into.at[k], seq=a_peer[k - 1]))
        total = message(0)
        fill[2]()
        for copy in stage:
            copy.wait_recv()
        for k in (1, 2, 3):
            total = total + mine(into, k)
        leave[...] = (we * total + ke * mine(own, c)).astype(BF16)
        swap = send(leave, entry.at[c], seq=partner)
        entry[c] = (wi * total + ki * mine(other)).astype(BF16)
        swap.wait_recv()

    act[:, 512:768] = acc[:, 512:768].astype(BF16)
    zk = acc[:, 256:512]
    act[:, 256:512] = (zk * sigmoid(zk)).astype(BF16)
    for h in range(HEADS):
        keys = act[:, head(1, h)].astype(F32) * fade[h]
        fs[h] = mm(keys.astype(BF16), act[:, head(2, h)], TN).astype(BF16)

    def queries():
        zq = acc[:, 0:256]
        act[:, 0:256] = (zq * sigmoid(zq)).astype(BF16)

    def local_scores(h):
        q, k, v = (act[:, head(p, h)] for p in range(3))
        p = (mm(q, k, NT) * mix[h]).astype(BF16)
        inside[h] = mm(p, v)
        sc[h] = (mm(k, q, NT) * mixt[h]).astype(BF16)
        qlt[h] = (q.astype(F32) * lead[h]).T.astype(BF16)

    exchange(
        fs, fo, fa, fm, fr, fe, fin, wtf,
        jnp.exp(fd * t1), jnp.exp(fc * t1), jnp.exp(fd * t0), fd, jnp.exp(fc * t0), fc,
        (queries, lambda: local_scores(0), lambda: local_scores(1)),
    )
    for h in range(HEADS):
        q = act[:, head(0, h)]
        attention = inside[h] + lead[h] * mm(q, fin[h])
        scale = jnp.sqrt(jnp.mean(attention * attention, axis=1, keepdims=True) + EPSILON)
        norm = attention / scale
        att_ref[:, h * HD:(h + 1) * HD] = norm.astype(BF16)
        up = cotv[:, h * HD:(h + 1) * HD].astype(F32)
        g = (up - norm * jnp.mean(up * norm, axis=1, keepdims=True)) / scale
        gout[h] = g.astype(BF16)
        bs[h] = mm(qlt[h], gout[h]).astype(BF16)

    def local_grads(h):
        q, k, v = (act[:, head(p, h)] for p in range(3))
        g = gout[h]
        through = (mm(g, v, NT) * mix[h]).astype(BF16)
        gq = mm(through, k) + lead[h] * mm(g, fin[h], NT)
        zq = acc[:, head(0, h)]
        sg = sigmoid(zq)
        grad[:, head(0, h)] = (gq * (sg * (1.0 + zq * (1.0 - sg)))).astype(BF16)
        through = (mm(v, g, NT) * mixt[h]).astype(BF16)
        gkv[h] = mm(through, q)
        gkv[2 + h] = mm(sc[h], g)
        zk = acc[:, head(1, h)]
        sg = sigmoid(zk)
        acc[:, head(1, h)] = sg * (1.0 + zk * (1.0 - sg))

    exchange(
        bs, bo, ba, bm, br, be, bin_, wtb,
        jnp.exp(fc * t0), jnp.exp(fd * t0), jnp.exp(fc * t1), fc, jnp.exp(fd * t1), fd,
        (lambda: None, lambda: local_grads(0), lambda: local_grads(1)),
    )
    for h in range(HEADS):
        future = bin_[h]
        k, v = act[:, head(1, h)], act[:, head(2, h)]
        gk = gkv[h] + fade[h] * mm(v, future, NT)
        grad[:, head(1, h)] = (gk * acc[:, head(1, h)]).astype(BF16)
        grad[:, head(2, h)] = (gkv[2 + h] + fade[h] * mm(k, future)).astype(BF16)

    def token_part(b):
        pbuf[b] = mm(grad[...], weight_block(b), NT).reshape(2, HALF, T)

    bufs_s, bufs_r = (sr, sl), (rrv, rlv)
    gz = {}

    def block_at(w, k):
        return lax.rem(z + (4 - k if w == 0 else 4 + k), NZ)

    def send_sum(w, k, h):
        val = pbuf[block_at(w, k), h]
        if k > 0 and (w, k - 1, h) in gz:
            gz[w, k - 1, h].wait_recv()
            val = val + bufs_r[w][k - 1, h].astype(F32)
        bufs_s[w][k, h] = val.astype(BF16)
        gz[w, k, h] = send(bufs_s[w].at[k, h], bufs_r[w].at[k, h], dp=way[w])

    far = lax.rem(z + 4, NZ)
    for h in (0, 1):
        rows = slice(h * HALF, (h + 1) * HALF)
        pbuf[far, h] = mm(grad[rows, :], weight_block(far), NT)
        send_sum(h, 0, h)

    def parts_far(i, zero):
        token_part(lax.rem(z + 3 + 2 * i, NZ))
        return zero

    lax.fori_loop(0, 2, parts_far, 0)
    send_sum(0, 1, 1)
    send_sum(1, 1, 0)

    def weight_part(b, zero):
        part = mm(tokb[b].reshape(T, T), grad[...], TN)
        pw[pl.ds(2 * b, 2)] = part.astype(BF16).reshape(2, 2, 128, 768)
        return zero

    gp = []
    for i in range(4):
        lax.fori_loop(2 * i, 2 * i + 2, weight_part, 0)
        gp.append(
            send(pw.at[4 * i:4 * i + 4, d], rpart.at[4 * i:4 * i + 4], seq=partner)
        )
    send_sum(0, 1, 0)
    send_sum(1, 1, 1)

    def chip_sum(i, zero):
        cs[i] = (pw[i, c].astype(F32) + rpart[i].astype(F32)).astype(BF16)
        return zero

    for i in range(4):
        gp[i].wait_recv()
        lax.fori_loop(4 * i, 4 * i + 4, chip_sum, 0)
    gb = []
    for k in (2, 1, 3):
        for m in range(4):
            src = (m * d + ring(x, k) * c) * NY + ring(y, k) * d + m * c
            gb.append(send(cs.at[src], rb.at[k - 1, m], seq=b_peer[k - 1]))

    def parts_near(i, zero):
        token_part(lax.rem(z + NZ - 2 + i, NZ))
        return zero

    lax.fori_loop(0, 5, parts_near, 0)
    send_sum(0, 2, 1)
    send_sum(1, 2, 0)
    send_sum(0, 2, 0)
    send_sum(1, 2, 1)
    send_sum(0, 3, 1)
    send_sum(1, 3, 0)
    send_sum(0, 3, 0)
    send_sum(1, 3, 1)
    for copy in gb:
        copy.wait_recv()
    for m in range(4):
        own = (m * d + x * c) * NY + y * d + m * c
        val = cs[own].astype(F32)
        for k in range(3):
            val = val + rb[k, m].astype(F32)
        dsum[m] = val.astype(BF16)
    at = x * d + y * c
    ga = [send(dsum.at[ring(at, k)], ra.at[k - 1], seq=a_peer[k - 1]) for k in (1, 2, 3)]
    for copy in ga:
        copy.wait_recv()
    val = dsum[at].astype(F32)
    for k in range(3):
        val = val + ra[k].astype(F32)
    val = (val * (1.0 / math.sqrt(16384.0))).astype(BF16)
    for p in range(3):
        gw_ref[p] = val[:, 256 * p:256 * (p + 1)]
    gz[0, 3, 1].wait_recv()
    gz[1, 3, 0].wait_recv()
    for h, ref in ((1, rrv), (0, rlv)):
        pbuf[z, h] += ref[3, h].astype(F32)
    gz[0, 3, 0].wait_recv()
    gz[1, 3, 1].wait_recv()
    for h, ref in ((0, rrv), (1, rlv)):
        gt_ref[h] = (pbuf[z, h] + ref[3, h].astype(F32)).astype(BF16)
    for copy in sent:
        copy.wait_send()
    assert len(sent) == COPIES, len(sent)


def hand_out(*refs):
    sems = refs[6]
    copies = [pltpu.make_async_copy(refs[i], refs[3 + i], sems.at[i]) for i in range(3)]
    for copy in copies:
        copy.start()
    for copy in copies:
        copy.wait()


def local(tokens, weights, log_decay, cotangent):
    vmem = pl.BlockSpec(memory_space=pltpu.VMEM)
    hbm = pl.BlockSpec(memory_space=pl.ANY)
    V = pltpu.VMEM
    states = [
        V((HEADS, HD, HD), BF16),
        V((HD, HD), BF16),
        V((4, HD, HD), BF16),
        V((4, HD, HD), BF16), V((4, HD, HD), BF16),
        V((HD, HD), BF16),
        V((HEADS, HD, HD), BF16),
    ]
    scratch = [
        V((NZ, 2, HALF, T), BF16),
        V((32, 128, 768), BF16),
        V((T, 256), BF16),
        V((HEADS, T), F32),
        V((T, 768), F32),
        V((T, 768), BF16),
        V((T, 768), BF16),
        V((HEADS, T, 128), F32),
        V((HEADS, 1, T), F32),
        V((HEADS, T, 128), F32), V((HEADS, T, 128), F32),
        V((HEADS, T, T), F32),
        V((HEADS, T, T), F32),
        V((HEADS, T, T), BF16),
        V((HEADS, T, HD), F32),
        V((HEADS, HD, T), BF16),
        V((HEADS, T, HD), BF16),
        V((4, T, HD), F32),
        V((2, HEADS, 8, 128), F32),
        V((16, HEADS, 8, 128), F32),
        V((16, 8, 128), F32), V((16, 8, 128), F32),
    ] + states + states + [
        V((NZ, 2, HALF, T), F32),
        V((4, 2, HALF, T), BF16), V((4, 2, HALF, T), BF16),
        V((4, 2, HALF, T), BF16), V((4, 2, HALF, T), BF16),
        V((16, 2, 128, 768), BF16),
        V((16, 128, 768), BF16),
        V((16, 128, 768), BF16),
        V((3, 4, 128, 768), BF16),
        V((4, 128, 768), BF16),
        V((3, 128, 768), BF16),
        pltpu.SemaphoreType.DMA((COPIES,)),
        pltpu.SemaphoreType.DMA((COPIES,)),
        pltpu.SemaphoreType.DMA((6,)),
    ]
    attended, grad_tokens, grad_weights = pl.pallas_call(
        kernel,
        out_shape=(
            pltpu.VMEM((T, 256), BF16),
            pltpu.VMEM((2, HALF, T), BF16),
            pltpu.VMEM((3, 128, 256), BF16),
        ),
        in_specs=[hbm] * 4,
        out_specs=(vmem,) * 3,
        scratch_shapes=scratch,
        compiler_params=pltpu.CompilerParams(
            collective_id=0, has_side_effects=True, vmem_limit_bytes=VMEM_LIMIT
        ),
        name="layer",
    )(tokens.reshape(2, HALF, T), weights.transpose(1, 0, 2), log_decay, cotangent)
    attended, grad_tokens, grad_weights = pl.pallas_call(
        hand_out,
        out_shape=(
            jax.ShapeDtypeStruct((T, 256), BF16),
            jax.ShapeDtypeStruct((2, HALF, T), BF16),
            jax.ShapeDtypeStruct((3, 128, 256), BF16),
        ),
        in_specs=[vmem] * 3,
        out_specs=(hbm,) * 3,
        scratch_shapes=[pltpu.SemaphoreType.DMA((3,))],
        compiler_params=pltpu.CompilerParams(vmem_limit_bytes=1 << 20),
        name="hand_out",
    )(attended, grad_tokens, grad_weights)
    return attended, grad_tokens.reshape(T, T), grad_weights.transpose(1, 0, 2)


def solution(mesh):
    return jax.shard_map(
        local,
        mesh=mesh,
        in_specs=(P("seq", "dp"), P("seq", None, "dp"), P("dp", "seq"), P("seq", "dp")),
        out_specs=(P("seq", "dp"), P("seq", "dp"), P("seq", None, "dp")),
        check_vma=False,
    )
```

```python
import functools
import math

import jax
import jax.numpy as jnp
from jax import lax
from jax.experimental import pallas as pl
from jax.experimental.pallas import tpu as pltpu
from jax.sharding import PartitionSpec as P

HD = 128
EPSILON = 1e-06
NX, NY, NC, NZ = 4, 4, 2, 8
T, HALF = 512, 256
HEADS = 2
BLK = 128
F32, BF16 = jnp.float32, jnp.bfloat16
MESH = pl.DeviceIdType.MESH
COPIES = 101
VMEM_LIMIT = 59800000

NT = (((1,), (1,)), ((), ()))
TN = (((0,), (0,)), ((), ()))


def mm(a, b, dims=(((1,), (0,)), ((), ()))):
    return lax.dot_general(a, b, dims, preferred_element_type=F32)


def sigmoid(v):
    return 1.0 / (1.0 + jnp.exp(-v))


def kernel(
    tok_ref, w_ref, ld_ref, cot_ref, att_ref, gt_ref, gw_ref,
    tokb, wb, cotv, ldv, acc, act, grad, rc, rr, lead, fade, mix, mixt, sc,
    inside, qlt, gout, gkv, ttc, tca, wtf, wtb,
    fs, fo, fa, fm, fr, fe, fin, bs, bo, ba, bm, br, be, bin_,
    pbuf, sr, sl, rrv, rlv, pw, rpart, cs, rb, dsum, ra,
    ssem, rsem, lsem,
):
    z = lax.axis_index("dp")
    s = lax.axis_index("seq")
    c = lax.rem(s, 2)
    y = lax.rem(lax.div(s, 2), 4)
    x = lax.div(s, 8)
    d = 1 - c
    zr, zl = lax.rem(z + 1, NZ), lax.rem(z + NZ - 1, NZ)

    def ring(v, k):
        return lax.rem(v + k, 4)

    def place(px, py, pc):
        return (px * NY + py) * NC + pc

    partner = place(x, y, d)
    x_peer = [place(ring(x, k), y, c) for k in (1, 2, 3)]
    y_peer = [place(x, ring(y, k), c) for k in (1, 2, 3)]
    a_peer = [place(ring(x, k * d), ring(y, k * c), c) for k in (1, 2, 3)]
    b_peer = [place(ring(x, k * c), ring(y, k * d), c) for k in (1, 2, 3)]

    here = [
        pltpu.make_async_copy(
            w_ref.at[p], wb.at[s, :, pl.ds(256 * p, 256)], lsem.at[p]
        )
        for p in range(3)
    ]
    here.append(pltpu.make_async_copy(tok_ref, tokb.at[z], lsem.at[3]))
    here.append(pltpu.make_async_copy(cot_ref, cotv, lsem.at[4]))
    here.append(pltpu.make_async_copy(ld_ref, ldv, lsem.at[5]))

    sent = []

    def send(src, dst, **dev):
        i = len(sent)
        copy = pltpu.make_async_remote_copy(
            src_ref=src, dst_ref=dst, send_sem=ssem.at[i], recv_sem=rsem.at[i],
            device_id=dev, device_id_type=MESH,
        )
        copy.start()
        sent.append((copy, None))
        return copy

    def send_if(needed, src, dst, peer):
        i = len(sent)
        copy = pltpu.make_async_remote_copy(
            src_ref=src, dst_ref=dst, send_sem=ssem.at[i], recv_sem=rsem.at[i],
            device_id={"seq": peer}, device_id_type=MESH,
        )
        pl.when(needed)(copy.start)
        sent.append((copy, needed))
        return copy

    for ref in (fa, fr, ba, br):
        ref[...] = jnp.zeros_like(ref)

    barrier = pltpu.get_barrier_semaphore()
    for peer in [partner] + x_peer + y_peer:
        pl.semaphore_signal(barrier, inc=1, device_id={"seq": peer}, device_id_type=MESH)
    for peer in (zr, zl):
        pl.semaphore_signal(barrier, inc=1, device_id={"dp": peer}, device_id_type=MESH)
    for copy in here:
        copy.start()
    pl.semaphore_wait(barrier, 9)

    first = (0, 1)
    way = (zr, zl)
    zc = {}
    here[3].wait()
    for h in (0, 1):
        for w in (0, 1):
            half = h if w == 0 else 1 - h
            zc[w, 0, half] = send(tokb.at[z, half], tokb.at[z, half], dp=way[w])
    for copy in here[:3]:
        copy.wait()
    wa = [send(wb.at[s], wb.at[s], seq=p) for p in a_peer]
    wp = [send(wb.at[s], wb.at[s], seq=partner)]

    here[5].wait()
    def decay_rows(i, total):
        h, b = lax.div(i, 4), lax.rem(i, 4)
        rows = pl.ds(pl.multiple_of(b * BLK, BLK), BLK)
        row_id = b * BLK + lax.broadcasted_iota(jnp.int32, (BLK, T), 0)
        col_id = lax.broadcasted_iota(jnp.int32, (BLK, T), 1)
        run = jnp.sum(jnp.where(col_id <= row_id, ldv[pl.ds(h, 1), :], 0.0), axis=1, keepdims=True)
        rc[h, rows, :] = jnp.broadcast_to(run, (BLK, BLK))
        return total

    lax.fori_loop(0, 8, decay_rows, 0)
    for h in range(HEADS):
        row = jnp.zeros((1, T), F32)
        for b in range(4):
            row_id = b * BLK + lax.broadcasted_iota(jnp.int32, (BLK, T), 0)
            col_id = lax.broadcasted_iota(jnp.int32, (BLK, T), 1)
            run = rc[h, b * BLK:(b + 1) * BLK, 0:1]
            row = row + jnp.sum(jnp.where(row_id == col_id, run, 0.0), axis=0, keepdims=True)
        rr[h] = row
        ttc[c, h] = rc[h, T - 8:T, :][7:8, :] + jnp.zeros((8, 128), F32)
    tc_copy = send(ttc.at[c], ttc.at[c], seq=partner)

    def mixing(i, zero):
        h, b = lax.div(i, 4), lax.rem(i, 4)
        rows = pl.ds(pl.multiple_of(b * BLK, BLK), BLK)
        row_id = b * BLK + lax.broadcasted_iota(jnp.int32, (BLK, T), 0)
        col_id = lax.broadcasted_iota(jnp.int32, (BLK, T), 1)
        spread = rc[h, rows, 0:1] - rr[h]
        mix[h, rows, :] = jnp.where(row_id >= col_id, jnp.exp(jnp.minimum(spread, 0.0)), 0.0)
        mixt[h, rows, :] = jnp.where(row_id <= col_id, jnp.exp(jnp.minimum(-spread, 0.0)), 0.0)
        lead[h, rows, :] = jnp.exp(rc[h, rows, :])
        fade[h, rows, :] = jnp.exp(ttc[c, h, 0:1, :] - rc[h, rows, :])
        return zero

    tc_copy.wait_recv()
    chip = x * NY + y
    tca[chip] = ttc[0] + ttc[1]
    ty_copy = [send(tca.at[chip], tca.at[chip], seq=p) for p in y_peer]

    for copy in wa:
        copy.wait_recv()
    wbc = []
    for k in (1, 2, 3):
        for m in range(4):
            src = place(m * d + x * c, y * d + m * c, c)
            wbc.append(send(wb.at[src], wb.at[src], seq=b_peer[k - 1]))
    for k in (1, 2, 3):
        src = place(ring(x, (4 - k) * d), ring(y, (4 - k) * c), c)
        wp.append(send(wb.at[src], wb.at[src], seq=partner))

    def pass_on(k):
        for half in (0, 1):
            for w in (0, 1):
                h = half if w == 0 else 1 - half
                if k == 3 and h != first[w]:
                    continue
                zc[w, k - 1, h].wait_recv()
                shard = lax.rem(z + (NZ - k if w == 0 else k), NZ)
                zc[w, k, h] = send(tokb.at[shard, h], tokb.at[shard, h], dp=way[w])

    def hand_over(k):
        for m in range(4):
            wbc[4 * (k - 1) + m].wait_recv()
        for m in range(4):
            back = 4 - k
            src = place(m * d + ring(x, back) * c, ring(y, back) * d + m * c, c)
            wp.append(send(wb.at[src], wb.at[src], seq=partner))

    pass_on(1)
    for copy in ty_copy:
        copy.wait_recv()
    line = pl.ds(NY * x, NY)
    tx_copy = [send(tca.at[line], tca.at[line], seq=p) for p in x_peer]
    lax.fori_loop(0, 8, mixing, 0)
    pass_on(2)
    hand_over(1)
    hand_over(3)
    for copy in tx_copy:
        copy.wait_recv()
    hand_over(2)

    def weigh(n, zero):
        k, i = lax.div(n, 4), lax.rem(n, 4)
        p = (x * d + i * c) * NY + i * d + y * c
        q = ring(x, k * d) * NY + ring(y, k * c)
        ahead = jnp.zeros((8, 128), F32)
        behind = jnp.zeros((8, 128), F32)
        for j in range(NX * NY):
            total = tca[j, c]
            ahead = ahead + jnp.logical_and(j > p, j < q).astype(F32) * total
            behind = behind + jnp.logical_and(j < p, j > q).astype(F32) * total
        wtf[n] = (p < q).astype(F32) * jnp.exp(ahead)
        wtb[n] = (p > q).astype(F32) * jnp.exp(behind)
        return zero

    lax.fori_loop(0, 16, weigh, 0)
    pass_on(3)
    here[4].wait()
    for copy in wp:
        copy.wait_recv()

    def weight_block(b):
        return wb[pl.ds(4 * b, 4)].reshape(T, 768)

    def project(b, start=False):
        part = mm(tokb[b].reshape(T, T), weight_block(b))
        if start:
            acc[...] = part
        else:
            acc[...] += part

    project(z, True)

    def project_near(i, zero):
        project(lax.rem(z + NZ - 2 + i + lax.div(i, 2), NZ))
        return zero

    lax.fori_loop(0, 4, project_near, 0)
    for w in (0, 1):
        zc[w, 2, 1 - first[w]].wait_recv()

    def project_far(i, zero):
        project(lax.rem(z + 3 + 2 * i, NZ))
        return zero

    lax.fori_loop(0, 2, project_far, 0)
    for w in (0, 1):
        zc[w, 3, first[w]].wait_recv()
    far = lax.rem(z + 4, NZ)
    acc[:, 256:768] += mm(
        tokb[far].reshape(T, T), wb[pl.ds(4 * far, 4), :, 256:768].reshape(T, 512)
    )

    def head(part, h):
        return pl.ds(pl.multiple_of(part * 256 + h * HD, HD), HD)

    def scalar(flag):
        return flag.astype(F32)

    t0, t1 = ttc[0, c, 0:1, :], ttc[1, c, 0:1, :]
    fc, fd = scalar(c), scalar(d)

    def mine(ref, j=None):
        return (ref[...] if j is None else ref[j]).astype(F32)

    def num(flag):
        return flag.astype(jnp.int32)

    def either(on0, on1):
        return d * on0 + c * on1 > 0

    forth, back = [[], []], [[], []]
    for k in (1, 2, 3):
        ty, tx, sy, sx = ring(y, k), ring(x, k), ring(y, 4 - k), ring(x, 4 - k)
        forth[0].append((
            either(num(x < 3) + num(ty > y), num(tx > x)),
            either(num(x < 3) + num(sy < y), num(sx < x)),
        ))
        forth[1].append((
            either(num(tx > x), num(x > 0) + num(ty > y)),
            either(num(sx < x), num(x > 0) + num(sy < y)),
        ))
        back[0].append((
            either(num(x > 0) + num(ty < y), num(tx < x)),
            either(num(x > 0) + num(sy > y), num(sx > x)),
        ))
        back[1].append((
            either(num(tx < x), num(x < 3) + num(ty < y)),
            either(num(sx > x), num(x < 3) + num(sy > y)),
        ))

    def exchange(needed, own, other, line, out, into, leave, entry, weights, wo, wp, we, ke, wi, ki, fill, use):
        swap = send(own.at[d], other, seq=partner)
        fill[0]()
        swap.wait_recv()
        at = y * d + x * c
        line[at] = (wo * mine(own, c) + wp * mine(other)).astype(BF16)
        stage = [
            (send_if(needed[0][k][0], line.at[at], line.at[at], b_peer[k]), needed[0][k][1])
            for k in (1, 0, 2)
        ]
        fill[1]()
        for copy, there in stage:
            pl.when(there)(copy.wait_recv)

        def message(k):
            val = weights[4 * k, 0:1, :] * mine(line, 0)
            for i in (1, 2, 3):
                val = val + weights[4 * k + i, 0:1, :] * mine(line, i)
            return val

        stage = []
        for k in (2, 1, 3):
            out[k] = message(k).astype(BF16)
            go, there = needed[1][k - 1]
            stage.append((send_if(go, out.at[k], into.at[k], a_peer[k - 1]), there))
        total = message(0)
        fill[2]()
        for copy, there in stage:
            pl.when(there)(copy.wait_recv)
        for k in (1, 2, 3):
            total = total + mine(into, k)
        leave[...] = (we * total + ke * mine(own, c)).astype(BF16)
        swap = send(leave, entry.at[c], seq=partner)
        entry[c] = (wi * total + ki * mine(other)).astype(BF16)
        use(c)
        swap.wait_recv()
        use(d)

    act[:, 512:768] = acc[:, 512:768].astype(BF16)
    zk = acc[:, 256:512]
    act[:, 256:512] = (zk * sigmoid(zk)).astype(BF16)
    for h in range(HEADS):
        keys = act[:, head(1, h)].astype(F32) * fade[h]
        fs[h] = mm(keys.astype(BF16), act[:, head(2, h)], TN).astype(BF16)

    def queries():
        zq = acc[:, 0:256] + mm(
            tokb[far].reshape(T, T), wb[pl.ds(4 * far, 4), :, 0:256].reshape(T, 256)
        )
        acc[:, 0:256] = zq
        act[:, 0:256] = (zq * sigmoid(zq)).astype(BF16)

    def local_scores(h):
        q, k, v = (act[:, head(p, h)] for p in range(3))
        p = (mm(q, k, NT) * mix[h]).astype(BF16)
        inside[h] = mm(p, v)
        sc[h] = (mm(k, q, NT) * mixt[h]).astype(BF16)
        qlt[h] = (q.astype(F32) * lead[h]).T.astype(BF16)

    def attend(h):
        q = act[:, head(0, h)]
        attention = inside[h] + lead[h] * mm(q, fin[h])
        scale = jnp.sqrt(jnp.mean(attention * attention, axis=1, keepdims=True) + EPSILON)
        norm = attention / scale
        att_ref[:, head(0, h)] = norm.astype(BF16)
        up = cotv[:, head(0, h)].astype(F32)
        g = (up - norm * jnp.mean(up * norm, axis=1, keepdims=True)) / scale
        gout[h] = g.astype(BF16)
        bs[h] = mm(qlt[h], gout[h]).astype(BF16)

    exchange(
        forth, fs, fo, fa, fm, fr, fe, fin, wtf,
        jnp.exp(fd * t1), jnp.exp(fc * t1), jnp.exp(fd * t0), fd, jnp.exp(fc * t0), fc,
        (queries, lambda: local_scores(0), lambda: local_scores(1)), attend,
    )

    def local_grads(h):
        q, k, v = (act[:, head(p, h)] for p in range(3))
        g = gout[h]
        through = (mm(g, v, NT) * mix[h]).astype(BF16)
        gq = mm(through, k) + lead[h] * mm(g, fin[h], NT)
        zq = acc[:, head(0, h)]
        sg = sigmoid(zq)
        grad[:, head(0, h)] = (gq * (sg * (1.0 + zq * (1.0 - sg)))).astype(BF16)
        through = (mm(v, g, NT) * mixt[h]).astype(BF16)
        gkv[h] = mm(through, q)
        gkv[2 + h] = mm(sc[h], g)
        zk = acc[:, head(1, h)]
        sg = sigmoid(zk)
        acc[:, head(1, h)] = sg * (1.0 + zk * (1.0 - sg))

    def last_grads(h):
        future = bin_[h]
        k, v = act[:, head(1, h)], act[:, head(2, h)]
        gk = gkv[h] + fade[h] * mm(v, future, NT)
        grad[:, head(1, h)] = (gk * acc[:, head(1, h)]).astype(BF16)
        grad[:, head(2, h)] = (gkv[2 + h] + fade[h] * mm(k, future)).astype(BF16)

    exchange(
        back, bs, bo, ba, bm, br, be, bin_, wtb,
        jnp.exp(fc * t0), jnp.exp(fd * t0), jnp.exp(fc * t1), fc, jnp.exp(fd * t1), fd,
        (lambda: None, lambda: local_grads(0), lambda: local_grads(1)), last_grads,
    )

    def token_part(b):
        pbuf[b] = mm(grad[...], weight_block(b), NT).reshape(2, HALF, T)

    bufs_s, bufs_r = (sr, sl), (rrv, rlv)
    gz = {}

    def block_at(w, k):
        return lax.rem(z + (4 - k if w == 0 else 4 + k), NZ)

    def send_sum(w, k, h):
        val = pbuf[block_at(w, k), h]
        if k > 0 and (w, k - 1, h) in gz:
            gz[w, k - 1, h].wait_recv()
            val = val + bufs_r[w][k - 1, h].astype(F32)
        bufs_s[w][k, h] = val.astype(BF16)
        gz[w, k, h] = send(bufs_s[w].at[k, h], bufs_r[w].at[k, h], dp=way[w])

    for h in (0, 1):
        rows = slice(h * HALF, (h + 1) * HALF)
        pbuf[far, h] = mm(grad[rows, :], weight_block(far), NT)
        send_sum(h, 0, h)

    def parts_far(i, zero):
        token_part(lax.rem(z + 3 + 2 * i, NZ))
        return zero

    lax.fori_loop(0, 2, parts_far, 0)
    send_sum(0, 1, 1)
    send_sum(1, 1, 0)

    def weight_part(b, zero):
        part = mm(tokb[b].reshape(T, T), grad[...], TN)
        pw[pl.ds(2 * b, 2)] = part.astype(BF16).reshape(2, 2, 128, 768)
        return zero

    gp = []
    for i in range(4):
        lax.fori_loop(2 * i, 2 * i + 2, weight_part, 0)
        gp.append(
            send(pw.at[4 * i:4 * i + 4, d], rpart.at[4 * i:4 * i + 4], seq=partner)
        )
    send_sum(0, 1, 0)
    send_sum(1, 1, 1)

    def chip_sum(i, zero):
        cs[i] = (pw[i, c].astype(F32) + rpart[i].astype(F32)).astype(BF16)
        return zero

    for i in range(4):
        gp[i].wait_recv()
        lax.fori_loop(4 * i, 4 * i + 4, chip_sum, 0)
    gb = []
    for k in (2, 1, 3):
        for m in range(4):
            src = (m * d + ring(x, k) * c) * NY + ring(y, k) * d + m * c
            gb.append(send(cs.at[src], rb.at[k - 1, m], seq=b_peer[k - 1]))

    def parts_near(i, zero):
        token_part(lax.rem(z + NZ - 2 + i, NZ))
        return zero

    lax.fori_loop(0, 5, parts_near, 0)
    send_sum(0, 2, 1)
    send_sum(1, 2, 0)
    send_sum(0, 2, 0)
    send_sum(1, 2, 1)
    send_sum(0, 3, 1)
    send_sum(1, 3, 0)
    send_sum(0, 3, 0)
    send_sum(1, 3, 1)
    for copy in gb:
        copy.wait_recv()
    for m in range(4):
        own = (m * d + x * c) * NY + y * d + m * c
        val = cs[own].astype(F32)
        for k in range(3):
            val = val + rb[k, m].astype(F32)
        dsum[m] = val.astype(BF16)
    at = x * d + y * c
    ga = [send(dsum.at[ring(at, k)], ra.at[k - 1], seq=a_peer[k - 1]) for k in (1, 2, 3)]
    for copy in ga:
        copy.wait_recv()
    val = dsum[at].astype(F32)
    for k in range(3):
        val = val + ra[k].astype(F32)
    val = (val * (1.0 / math.sqrt(16384.0))).astype(BF16)
    for p in range(3):
        gw_ref[p] = val[:, 256 * p:256 * (p + 1)]
    gz[0, 3, 1].wait_recv()
    gz[1, 3, 0].wait_recv()
    for h, ref in ((1, rrv), (0, rlv)):
        pbuf[z, h] += ref[3, h].astype(F32)
    gz[0, 3, 0].wait_recv()
    gz[1, 3, 1].wait_recv()
    for h, ref in ((0, rrv), (1, rlv)):
        gt_ref[h] = (pbuf[z, h] + ref[3, h].astype(F32)).astype(BF16)
    for copy, needed in sent:
        if needed is None:
            copy.wait_send()
        else:
            pl.when(needed)(copy.wait_send)
    assert len(sent) == COPIES, len(sent)


def hand_out(*refs):
    sems = refs[6]
    copies = [pltpu.make_async_copy(refs[i], refs[3 + i], sems.at[i]) for i in range(3)]
    for copy in copies:
        copy.start()
    for copy in copies:
        copy.wait()


def local(tokens, weights, log_decay, cotangent):
    vmem = pl.BlockSpec(memory_space=pltpu.VMEM)
    hbm = pl.BlockSpec(memory_space=pl.ANY)
    V = pltpu.VMEM
    states = [
        V((HEADS, HD, HD), BF16),
        V((HD, HD), BF16),
        V((4, HD, HD), BF16),
        V((4, HD, HD), BF16), V((4, HD, HD), BF16),
        V((HD, HD), BF16),
        V((HEADS, HD, HD), BF16),
    ]
    scratch = [
        V((NZ, 2, HALF, T), BF16),
        V((32, 128, 768), BF16),
        V((T, 256), BF16),
        V((HEADS, T), F32),
        V((T, 768), F32),
        V((T, 768), BF16),
        V((T, 768), BF16),
        V((HEADS, T, 128), F32),
        V((HEADS, 1, T), F32),
        V((HEADS, T, 128), F32), V((HEADS, T, 128), F32),
        V((HEADS, T, T), F32),
        V((HEADS, T, T), F32),
        V((HEADS, T, T), BF16),
        V((HEADS, T, HD), F32),
        V((HEADS, HD, T), BF16),
        V((HEADS, T, HD), BF16),
        V((4, T, HD), F32),
        V((2, HEADS, 8, 128), F32),
        V((16, HEADS, 8, 128), F32),
        V((16, 8, 128), F32), V((16, 8, 128), F32),
    ] + states + states + [
        V((NZ, 2, HALF, T), F32),
        V((4, 2, HALF, T), BF16), V((4, 2, HALF, T), BF16),
        V((4, 2, HALF, T), BF16), V((4, 2, HALF, T), BF16),
        V((16, 2, 128, 768), BF16),
        V((16, 128, 768), BF16),
        V((16, 128, 768), BF16),
        V((3, 4, 128, 768), BF16),
        V((4, 128, 768), BF16),
        V((3, 128, 768), BF16),
        pltpu.SemaphoreType.DMA((COPIES,)),
        pltpu.SemaphoreType.DMA((COPIES,)),
        pltpu.SemaphoreType.DMA((6,)),
    ]
    attended, grad_tokens, grad_weights = pl.pallas_call(
        kernel,
        out_shape=(
            pltpu.VMEM((T, 256), BF16),
            pltpu.VMEM((2, HALF, T), BF16),
            pltpu.VMEM((3, 128, 256), BF16),
        ),
        in_specs=[hbm] * 4,
        out_specs=(vmem,) * 3,
        scratch_shapes=scratch,
        compiler_params=pltpu.CompilerParams(
            collective_id=0, has_side_effects=True, vmem_limit_bytes=VMEM_LIMIT
        ),
        name="layer",
    )(tokens.reshape(2, HALF, T), weights.transpose(1, 0, 2), log_decay, cotangent)
    attended, grad_tokens, grad_weights = pl.pallas_call(
        hand_out,
        out_shape=(
            jax.ShapeDtypeStruct((T, 256), BF16),
            jax.ShapeDtypeStruct((2, HALF, T), BF16),
            jax.ShapeDtypeStruct((3, 128, 256), BF16),
        ),
        in_specs=[vmem] * 3,
        out_specs=(hbm,) * 3,
        scratch_shapes=[pltpu.SemaphoreType.DMA((3,))],
        compiler_params=pltpu.CompilerParams(vmem_limit_bytes=1 << 20),
        name="hand_out",
    )(attended, grad_tokens, grad_weights)
    return attended, grad_tokens.reshape(T, T), grad_weights.transpose(1, 0, 2)


def solution(mesh):
    return jax.shard_map(
        local,
        mesh=mesh,
        in_specs=(P("seq", "dp"), P("seq", None, "dp"), P("dp", "seq"), P("seq", "dp")),
        out_specs=(P("seq", "dp"), P("seq", "dp"), P("seq", None, "dp")),
        check_vma=False,
    )
```

```python
import functools
import math

import jax
import jax.numpy as jnp
from jax import lax
from jax.experimental import pallas as pl
from jax.experimental.pallas import tpu as pltpu
from jax.sharding import PartitionSpec as P

HD = 128
EPSILON = 1e-06
NX, NY, NC, NZ = 4, 4, 2, 8
T, HALF = 512, 256
HEADS = 2
BLK = 128
F32, BF16 = jnp.float32, jnp.bfloat16
MESH = pl.DeviceIdType.MESH
COPIES = 107
VMEM_LIMIT = 59800000

NT = (((1,), (1,)), ((), ()))
TN = (((0,), (0,)), ((), ()))


def mm(a, b, dims=(((1,), (0,)), ((), ()))):
    return lax.dot_general(a, b, dims, preferred_element_type=F32)


def sigmoid(v):
    return 1.0 / (1.0 + jnp.exp(-v))


def kernel(
    tok_ref, w_ref, ld_ref, cot_ref, att_ref, gt_ref, gw_ref,
    tokb, wb, cotv, ldv, acc, act, grad, rc, rr, lead, fade, mix, mixt, sc,
    inside, qlt, gout, gkv, ttc, tca, wtf, wtb,
    fs, fo, fa, fm, fr, fz, fin, bs, bo, ba, bm, br, bz, bin_,
    pbuf, sr, sl, rrv, rlv, pw, rpart, cs, rb, dsum, ra,
    ssem, rsem, lsem,
):
    z = lax.axis_index("dp")
    s = lax.axis_index("seq")
    c = lax.rem(s, 2)
    y = lax.rem(lax.div(s, 2), 4)
    x = lax.div(s, 8)
    d = 1 - c
    zr, zl = lax.rem(z + 1, NZ), lax.rem(z + NZ - 1, NZ)

    def ring(v, k):
        return lax.rem(v + k, 4)

    def place(px, py, pc):
        return (px * NY + py) * NC + pc

    partner = place(x, y, d)
    x_peer = [place(ring(x, k), y, c) for k in (1, 2, 3)]
    y_peer = [place(x, ring(y, k), c) for k in (1, 2, 3)]
    a_peer = [place(ring(x, k * d), ring(y, k * c), c) for k in (1, 2, 3)]
    b_peer = [place(ring(x, k * c), ring(y, k * d), c) for k in (1, 2, 3)]

    here = [
        pltpu.make_async_copy(
            w_ref.at[p], wb.at[s, :, pl.ds(256 * p, 256)], lsem.at[p]
        )
        for p in range(3)
    ]
    here.append(pltpu.make_async_copy(tok_ref, tokb.at[z], lsem.at[3]))
    here.append(pltpu.make_async_copy(cot_ref, cotv, lsem.at[4]))
    here.append(pltpu.make_async_copy(ld_ref, ldv, lsem.at[5]))

    sent = []

    def send(src, dst, **dev):
        i = len(sent)
        copy = pltpu.make_async_remote_copy(
            src_ref=src, dst_ref=dst, send_sem=ssem.at[i], recv_sem=rsem.at[i],
            device_id=dev, device_id_type=MESH,
        )
        copy.start()
        sent.append((copy, None))
        return copy

    def send_if(needed, src, dst, peer):
        i = len(sent)
        copy = pltpu.make_async_remote_copy(
            src_ref=src, dst_ref=dst, send_sem=ssem.at[i], recv_sem=rsem.at[i],
            device_id={"seq": peer}, device_id_type=MESH,
        )
        pl.when(needed)(copy.start)
        sent.append((copy, needed))
        return copy

    for ref in (fa, fr, ba, br):
        ref[...] = jnp.zeros_like(ref)

    barrier = pltpu.get_barrier_semaphore()
    for peer in [partner] + x_peer + y_peer:
        pl.semaphore_signal(barrier, inc=1, device_id={"seq": peer}, device_id_type=MESH)
    for peer in (zr, zl):
        pl.semaphore_signal(barrier, inc=1, device_id={"dp": peer}, device_id_type=MESH)
    for copy in here:
        copy.start()
    pl.semaphore_wait(barrier, 9)

    first = (0, 1)
    way = (zr, zl)
    zc = {}
    here[3].wait()
    for h in (0, 1):
        for w in (0, 1):
            half = h if w == 0 else 1 - h
            zc[w, 0, half] = send(tokb.at[z, half], tokb.at[z, half], dp=way[w])
    for copy in here[:3]:
        copy.wait()
    wa = [send(wb.at[s], wb.at[s], seq=p) for p in a_peer]
    wp = [send(wb.at[s], wb.at[s], seq=partner)]

    here[5].wait()
    def decay_rows(i, total):
        h, b = lax.div(i, 4), lax.rem(i, 4)
        rows = pl.ds(pl.multiple_of(b * BLK, BLK), BLK)
        row_id = b * BLK + lax.broadcasted_iota(jnp.int32, (BLK, T), 0)
        col_id = lax.broadcasted_iota(jnp.int32, (BLK, T), 1)
        run = jnp.sum(jnp.where(col_id <= row_id, ldv[pl.ds(h, 1), :], 0.0), axis=1, keepdims=True)
        rc[h, rows, :] = jnp.broadcast_to(run, (BLK, BLK))
        return total

    lax.fori_loop(0, 8, decay_rows, 0)
    for h in range(HEADS):
        row = jnp.zeros((1, T), F32)
        for b in range(4):
            row_id = b * BLK + lax.broadcasted_iota(jnp.int32, (BLK, T), 0)
            col_id = lax.broadcasted_iota(jnp.int32, (BLK, T), 1)
            run = rc[h, b * BLK:(b + 1) * BLK, 0:1]
            row = row + jnp.sum(jnp.where(row_id == col_id, run, 0.0), axis=0, keepdims=True)
        rr[h] = row
        ttc[c, h] = rc[h, T - 8:T, :][7:8, :] + jnp.zeros((8, 128), F32)
    tc_copy = send(ttc.at[c], ttc.at[c], seq=partner)

    def mixing(i, zero):
        h, b = lax.div(i, 4), lax.rem(i, 4)
        rows = pl.ds(pl.multiple_of(b * BLK, BLK), BLK)
        row_id = b * BLK + lax.broadcasted_iota(jnp.int32, (BLK, T), 0)
        col_id = lax.broadcasted_iota(jnp.int32, (BLK, T), 1)
        spread = rc[h, rows, 0:1] - rr[h]
        mix[h, rows, :] = jnp.where(row_id >= col_id, jnp.exp(jnp.minimum(spread, 0.0)), 0.0)
        mixt[h, rows, :] = jnp.where(row_id <= col_id, jnp.exp(jnp.minimum(-spread, 0.0)), 0.0)
        lead[h, rows, :] = jnp.exp(rc[h, rows, :])
        fade[h, rows, :] = jnp.exp(ttc[c, h, 0:1, :] - rc[h, rows, :])
        return zero

    tc_copy.wait_recv()
    chip = x * NY + y
    tca[chip] = ttc[0] + ttc[1]
    ty_copy = [send(tca.at[chip], tca.at[chip], seq=p) for p in y_peer]

    for copy in wa:
        copy.wait_recv()
    wbc = []
    for k in (1, 2, 3):
        for m in range(4):
            src = place(m * d + x * c, y * d + m * c, c)
            wbc.append(send(wb.at[src], wb.at[src], seq=b_peer[k - 1]))
    for k in (1, 2, 3):
        src = place(ring(x, (4 - k) * d), ring(y, (4 - k) * c), c)
        wp.append(send(wb.at[src], wb.at[src], seq=partner))

    def pass_on(k):
        for half in (0, 1):
            for w in (0, 1):
                h = half if w == 0 else 1 - half
                if k == 3 and h != first[w]:
                    continue
                zc[w, k - 1, h].wait_recv()
                shard = lax.rem(z + (NZ - k if w == 0 else k), NZ)
                zc[w, k, h] = send(tokb.at[shard, h], tokb.at[shard, h], dp=way[w])

    def hand_over(k):
        for m in range(4):
            wbc[4 * (k - 1) + m].wait_recv()
        for m in range(4):
            back = 4 - k
            src = place(m * d + ring(x, back) * c, ring(y, back) * d + m * c, c)
            wp.append(send(wb.at[src], wb.at[src], seq=partner))

    pass_on(1)
    for copy in ty_copy:
        copy.wait_recv()
    line = pl.ds(NY * x, NY)
    tx_copy = [send(tca.at[line], tca.at[line], seq=p) for p in x_peer]
    lax.fori_loop(0, 8, mixing, 0)
    pass_on(2)
    hand_over(1)
    hand_over(3)
    for copy in tx_copy:
        copy.wait_recv()
    hand_over(2)

    def weigh(n, zero):
        k, i = lax.div(n, 4), lax.rem(n, 4)
        p = (x * d + i * c) * NY + i * d + y * c
        q = ring(x, k * d) * NY + ring(y, k * c)
        ahead = jnp.zeros((8, 128), F32)
        behind = jnp.zeros((8, 128), F32)
        for j in range(NX * NY):
            total = tca[j, c]
            ahead = ahead + jnp.logical_and(j > p, j < q).astype(F32) * total
            behind = behind + jnp.logical_and(j < p, j > q).astype(F32) * total
        wtf[n] = (p < q).astype(F32) * jnp.exp(ahead)
        wtb[n] = (p > q).astype(F32) * jnp.exp(behind)
        return zero

    lax.fori_loop(0, 16, weigh, 0)
    pass_on(3)
    here[4].wait()
    for copy in wp:
        copy.wait_recv()

    def weight_block(b):
        return wb[pl.ds(4 * b, 4)].reshape(T, 768)

    def project(b, start=False):
        part = mm(tokb[b].reshape(T, T), weight_block(b))
        if start:
            acc[...] = part
        else:
            acc[...] += part

    project(z, True)

    def project_near(i, zero):
        project(lax.rem(z + NZ - 2 + i + lax.div(i, 2), NZ))
        return zero

    lax.fori_loop(0, 4, project_near, 0)
    for w in (0, 1):
        zc[w, 2, 1 - first[w]].wait_recv()

    def project_far(i, zero):
        project(lax.rem(z + 3 + 2 * i, NZ))
        return zero

    lax.fori_loop(0, 2, project_far, 0)
    for w in (0, 1):
        zc[w, 3, first[w]].wait_recv()
    far = lax.rem(z + 4, NZ)
    acc[:, 256:768] += mm(
        tokb[far].reshape(T, T), wb[pl.ds(4 * far, 4), :, 256:768].reshape(T, 512)
    )

    def head(part, h):
        return pl.ds(pl.multiple_of(part * 256 + h * HD, HD), HD)

    def scalar(flag):
        return flag.astype(F32)

    t0, t1 = ttc[0, c, 0:1, :], ttc[1, c, 0:1, :]
    fc, fd = scalar(c), scalar(d)

    def mine(ref, j=None):
        return (ref[...] if j is None else ref[j]).astype(F32)

    def num(flag):
        return flag.astype(jnp.int32)

    def either(on0, on1):
        return d * on0 + c * on1 > 0

    forth, back = [[], []], [[], []]
    for k in (1, 2, 3):
        ty, tx, sy, sx = ring(y, k), ring(x, k), ring(y, 4 - k), ring(x, 4 - k)
        forth[0].append((
            either(num(x < 3) + num(ty > y), num(tx > x)),
            either(num(x < 3) + num(sy < y), num(sx < x)),
        ))
        on0, on1 = num(sx < x), num(x > 0) + num(sy < y)
        forth[1].append((
            either(num(tx > x), num(x > 0) + num(ty > y)), either(on0, on1), either(on1, on0)
        ))
        back[0].append((
            either(num(x > 0) + num(ty < y), num(tx < x)),
            either(num(x > 0) + num(sy > y), num(sx > x)),
        ))
        on0, on1 = num(sx > x), num(x < 3) + num(sy > y)
        back[1].append((
            either(num(tx < x), num(x < 3) + num(ty < y)), either(on0, on1), either(on1, on0)
        ))
    across = [place(ring(x, k * d), ring(y, k * c), d) for k in (1, 2, 3)]

    def exchange(needed, own, other, line, out, into, mid, entry, weights, wo, wp, f, side, fill, use):
        swap = send(own, other, seq=partner)
        fill[0]()
        swap.wait_recv()
        at = y * d + x * c
        line[at] = (wo * mine(own, c) + wp * mine(other, c)).astype(BF16)
        stage = [
            (send_if(needed[0][k][0], line.at[at], line.at[at], b_peer[k]), needed[0][k][1])
            for k in (1, 0, 2)
        ]
        fill[1]()
        for copy, there in stage:
            pl.when(there)(copy.wait_recv)

        def message(k):
            val = weights[4 * k, 0:1, :] * mine(line, 0)
            for i in (1, 2, 3):
                val = val + weights[4 * k + i, 0:1, :] * mine(line, i)
            return val

        near, far_side = [], []
        for k in (2, 1, 3):
            out[k] = message(k).astype(BF16)
            go, there, there_too = needed[1][k - 1]
            near.append((send_if(go, out.at[k], into.at[c, k], a_peer[k - 1]), there))
            far_side.append((send_if(go, out.at[k], into.at[c, k], across[k - 1]), there_too))
        mid[c] = message(0).astype(BF16)
        swap = send(mid.at[c], mid.at[c], seq=partner)
        fill[2]()

        def enter(h):
            total = mine(mid, h)
            for k in (1, 2, 3):
                total = total + into[h, k].astype(F32)
            total = jnp.exp(f * ttc[side, h, 0:1, :]) * total
            entry[h] = (total + f * mine(other, h)).astype(BF16)
            use(h)

        for copy, there in near:
            pl.when(there)(copy.wait_recv)
        enter(c)
        swap.wait_recv()
        for copy, there in far_side:
            pl.when(there)(copy.wait_recv)
        enter(d)

    act[:, 512:768] = acc[:, 512:768].astype(BF16)
    zk = acc[:, 256:512]
    act[:, 256:512] = (zk * sigmoid(zk)).astype(BF16)
    for h in range(HEADS):
        keys = act[:, head(1, h)].astype(F32) * fade[h]
        fs[h] = mm(keys.astype(BF16), act[:, head(2, h)], TN).astype(BF16)

    def queries():
        zq = acc[:, 0:256] + mm(
            tokb[far].reshape(T, T), wb[pl.ds(4 * far, 4), :, 0:256].reshape(T, 256)
        )
        acc[:, 0:256] = zq
        act[:, 0:256] = (zq * sigmoid(zq)).astype(BF16)

    def local_scores(h):
        q, k, v = (act[:, head(p, h)] for p in range(3))
        p = (mm(q, k, NT) * mix[h]).astype(BF16)
        inside[h] = mm(p, v)
        sc[h] = (mm(k, q, NT) * mixt[h]).astype(BF16)
        qlt[h] = (q.astype(F32) * lead[h]).T.astype(BF16)

    def attend(h):
        q = act[:, head(0, h)]
        attention = inside[h] + lead[h] * mm(q, fin[h])
        scale = jnp.sqrt(jnp.mean(attention * attention, axis=1, keepdims=True) + EPSILON)
        norm = attention / scale
        att_ref[:, head(0, h)] = norm.astype(BF16)
        up = cotv[:, head(0, h)].astype(F32)
        g = (up - norm * jnp.mean(up * norm, axis=1, keepdims=True)) / scale
        gout[h] = g.astype(BF16)
        bs[h] = mm(qlt[h], gout[h]).astype(BF16)

    exchange(
        forth, fs, fo, fa, fm, fr, fz, fin, wtf, jnp.exp(fd * t1), jnp.exp(fc * t1), fc, 0,
        (queries, lambda: local_scores(0), lambda: local_scores(1)), attend,
    )

    def local_grads(h):
        q, k, v = (act[:, head(p, h)] for p in range(3))
        g = gout[h]
        through = (mm(g, v, NT) * mix[h]).astype(BF16)
        gq = mm(through, k) + lead[h] * mm(g, fin[h], NT)
        zq = acc[:, head(0, h)]
        sg = sigmoid(zq)
        grad[:, head(0, h)] = (gq * (sg * (1.0 + zq * (1.0 - sg)))).astype(BF16)
        through = (mm(v, g, NT) * mixt[h]).astype(BF16)
        gkv[h] = mm(through, q)
        gkv[2 + h] = mm(sc[h], g)
        zk = acc[:, head(1, h)]
        sg = sigmoid(zk)
        acc[:, head(1, h)] = sg * (1.0 + zk * (1.0 - sg))

    def last_grads(h):
        future = bin_[h]
        k, v = act[:, head(1, h)], act[:, head(2, h)]
        gk = gkv[h] + fade[h] * mm(v, future, NT)
        grad[:, head(1, h)] = (gk * acc[:, head(1, h)]).astype(BF16)
        grad[:, head(2, h)] = (gkv[2 + h] + fade[h] * mm(k, future)).astype(BF16)

    exchange(
        back, bs, bo, ba, bm, br, bz, bin_, wtb, jnp.exp(fc * t0), jnp.exp(fd * t0), fd, 1,
        (lambda: None, lambda: local_grads(0), lambda: local_grads(1)), last_grads,
    )

    def token_part(b):
        pbuf[b] = mm(grad[...], weight_block(b), NT).reshape(2, HALF, T)

    bufs_s, bufs_r = (sr, sl), (rrv, rlv)
    gz = {}

    def block_at(w, k):
        return lax.rem(z + (4 - k if w == 0 else 4 + k), NZ)

    def send_sum(w, k, h):
        val = pbuf[block_at(w, k), h]
        if k > 0 and (w, k - 1, h) in gz:
            gz[w, k - 1, h].wait_recv()
            val = val + bufs_r[w][k - 1, h].astype(F32)
        bufs_s[w][k, h] = val.astype(BF16)
        gz[w, k, h] = send(bufs_s[w].at[k, h], bufs_r[w].at[k, h], dp=way[w])

    for h in (0, 1):
        rows = slice(h * HALF, (h + 1) * HALF)
        pbuf[far, h] = mm(grad[rows, :], weight_block(far), NT)
        send_sum(h, 0, h)

    def parts_far(i, zero):
        token_part(lax.rem(z + 3 + 2 * i, NZ))
        return zero

    lax.fori_loop(0, 2, parts_far, 0)
    send_sum(0, 1, 1)
    send_sum(1, 1, 0)

    def weight_part(b, zero):
        part = mm(tokb[b].reshape(T, T), grad[...], TN)
        pw[pl.ds(2 * b, 2)] = part.astype(BF16).reshape(2, 2, 128, 768)
        return zero

    gp = []
    for i in range(4):
        lax.fori_loop(2 * i, 2 * i + 2, weight_part, 0)
        gp.append(
            send(pw.at[4 * i:4 * i + 4, d], rpart.at[4 * i:4 * i + 4], seq=partner)
        )
    send_sum(0, 1, 0)
    send_sum(1, 1, 1)

    def chip_sum(i, zero):
        cs[i] = (pw[i, c].astype(F32) + rpart[i].astype(F32)).astype(BF16)
        return zero

    for i in range(4):
        gp[i].wait_recv()
        lax.fori_loop(4 * i, 4 * i + 4, chip_sum, 0)
    gb = []
    for k in (2, 1, 3):
        for m in range(4):
            src = (m * d + ring(x, k) * c) * NY + ring(y, k) * d + m * c
            gb.append(send(cs.at[src], rb.at[k - 1, m], seq=b_peer[k - 1]))

    def parts_near(i, zero):
        token_part(lax.rem(z + NZ - 2 + i, NZ))
        return zero

    lax.fori_loop(0, 5, parts_near, 0)
    send_sum(0, 2, 1)
    send_sum(1, 2, 0)
    send_sum(0, 2, 0)
    send_sum(1, 2, 1)
    send_sum(0, 3, 1)
    send_sum(1, 3, 0)
    send_sum(0, 3, 0)
    send_sum(1, 3, 1)
    for copy in gb:
        copy.wait_recv()
    for m in range(4):
        own = (m * d + x * c) * NY + y * d + m * c
        val = cs[own].astype(F32)
        for k in range(3):
            val = val + rb[k, m].astype(F32)
        dsum[m] = val.astype(BF16)
    at = x * d + y * c
    ga = [send(dsum.at[ring(at, k)], ra.at[k - 1], seq=a_peer[k - 1]) for k in (1, 2, 3)]
    for copy in ga:
        copy.wait_recv()
    val = dsum[at].astype(F32)
    for k in range(3):
        val = val + ra[k].astype(F32)
    val = (val * (1.0 / math.sqrt(16384.0))).astype(BF16)
    for p in range(3):
        gw_ref[p] = val[:, 256 * p:256 * (p + 1)]
    gz[0, 3, 1].wait_recv()
    gz[1, 3, 0].wait_recv()
    for h, ref in ((1, rrv), (0, rlv)):
        pbuf[z, h] += ref[3, h].astype(F32)
    gz[0, 3, 0].wait_recv()
    gz[1, 3, 1].wait_recv()
    for h, ref in ((0, rrv), (1, rlv)):
        gt_ref[h] = (pbuf[z, h] + ref[3, h].astype(F32)).astype(BF16)
    for copy, needed in sent:
        if needed is None:
            copy.wait_send()
        else:
            pl.when(needed)(copy.wait_send)
    assert len(sent) == COPIES, len(sent)


def hand_out(*refs):
    sems = refs[6]
    copies = [pltpu.make_async_copy(refs[i], refs[3 + i], sems.at[i]) for i in range(3)]
    for copy in copies:
        copy.start()
    for copy in copies:
        copy.wait()


def local(tokens, weights, log_decay, cotangent):
    vmem = pl.BlockSpec(memory_space=pltpu.VMEM)
    hbm = pl.BlockSpec(memory_space=pl.ANY)
    V = pltpu.VMEM
    states = [
        V((HEADS, HD, HD), BF16),
        V((HEADS, HD, HD), BF16),
        V((4, HD, HD), BF16),
        V((4, HD, HD), BF16), V((HEADS, 4, HD, HD), BF16),
        V((HEADS, HD, HD), BF16),
        V((HEADS, HD, HD), BF16),
    ]
    scratch = [
        V((NZ, 2, HALF, T), BF16),
        V((32, 128, 768), BF16),
        V((T, 256), BF16),
        V((HEADS, T), F32),
        V((T, 768), F32),
        V((T, 768), BF16),
        V((T, 768), BF16),
        V((HEADS, T, 128), F32),
        V((HEADS, 1, T), F32),
        V((HEADS, T, 128), F32), V((HEADS, T, 128), F32),
        V((HEADS, T, T), F32),
        V((HEADS, T, T), F32),
        V((HEADS, T, T), BF16),
        V((HEADS, T, HD), F32),
        V((HEADS, HD, T), BF16),
        V((HEADS, T, HD), BF16),
        V((4, T, HD), F32),
        V((2, HEADS, 8, 128), F32),
        V((16, HEADS, 8, 128), F32),
        V((16, 8, 128), F32), V((16, 8, 128), F32),
    ] + states + states + [
        V((NZ, 2, HALF, T), F32),
        V((4, 2, HALF, T), BF16), V((4, 2, HALF, T), BF16),
        V((4, 2, HALF, T), BF16), V((4, 2, HALF, T), BF16),
        V((16, 2, 128, 768), BF16),
        V((16, 128, 768), BF16),
        V((16, 128, 768), BF16),
        V((3, 4, 128, 768), BF16),
        V((4, 128, 768), BF16),
        V((3, 128, 768), BF16),
        pltpu.SemaphoreType.DMA((COPIES,)),
        pltpu.SemaphoreType.DMA((COPIES,)),
        pltpu.SemaphoreType.DMA((6,)),
    ]
    attended, grad_tokens, grad_weights = pl.pallas_call(
        kernel,
        out_shape=(
            pltpu.VMEM((T, 256), BF16),
            pltpu.VMEM((2, HALF, T), BF16),
            pltpu.VMEM((3, 128, 256), BF16),
        ),
        in_specs=[hbm] * 4,
        out_specs=(vmem,) * 3,
        scratch_shapes=scratch,
        compiler_params=pltpu.CompilerParams(
            collective_id=0, has_side_effects=True, vmem_limit_bytes=VMEM_LIMIT
        ),
        name="layer",
    )(tokens.reshape(2, HALF, T), weights.transpose(1, 0, 2), log_decay, cotangent)
    attended, grad_tokens, grad_weights = pl.pallas_call(
        hand_out,
        out_shape=(
            jax.ShapeDtypeStruct((T, 256), BF16),
            jax.ShapeDtypeStruct((2, HALF, T), BF16),
            jax.ShapeDtypeStruct((3, 128, 256), BF16),
        ),
        in_specs=[vmem] * 3,
        out_specs=(hbm,) * 3,
        scratch_shapes=[pltpu.SemaphoreType.DMA((3,))],
        compiler_params=pltpu.CompilerParams(vmem_limit_bytes=1 << 20),
        name="hand_out",
    )(attended, grad_tokens, grad_weights)
    return attended, grad_tokens.reshape(T, T), grad_weights.transpose(1, 0, 2)


def solution(mesh):
    return jax.shard_map(
        local,
        mesh=mesh,
        in_specs=(P("seq", "dp"), P("seq", None, "dp"), P("dp", "seq"), P("seq", "dp")),
        out_specs=(P("seq", "dp"), P("seq", "dp"), P("seq", None, "dp")),
        check_vma=False,
    )
```

```python
import functools
import math

import jax
import jax.numpy as jnp
from jax import lax
from jax.experimental import pallas as pl
from jax.experimental.pallas import tpu as pltpu
from jax.sharding import PartitionSpec as P

HD = 128
EPSILON = 1e-06
NX, NY, NC, NZ = 4, 4, 2, 8
T, HALF = 512, 256
HEADS = 2
BLK = 128
F32, BF16 = jnp.float32, jnp.bfloat16
MESH = pl.DeviceIdType.MESH
COPIES = 107
VMEM_LIMIT = 59800000

NT = (((1,), (1,)), ((), ()))
TN = (((0,), (0,)), ((), ()))


def mm(a, b, dims=(((1,), (0,)), ((), ()))):
    return lax.dot_general(a, b, dims, preferred_element_type=F32)


def sigmoid(v):
    return 1.0 / (1.0 + jnp.exp(-v))


def kernel(
    tok_ref, w_ref, ld_ref, cot_ref, att_ref, gt_ref, gw_ref,
    tokb, wb, cotv, ldv, acc, act, grad, rc, rr, lead, fade, mix, mixt, sc,
    inside, qlt, gout, gkv, ttc, tca, wtf, wtb,
    fs, fo, fa, fm, fr, fz, fin, bs, bo, ba, bm, br, bz, bin_,
    pbuf, sr, sl, rrv, rlv, pw, rpart, cs, rb, dsum, ra,
    ssem, rsem, lsem,
):
    z = lax.axis_index("dp")
    s = lax.axis_index("seq")
    c = lax.rem(s, 2)
    y = lax.rem(lax.div(s, 2), 4)
    x = lax.div(s, 8)
    d = 1 - c
    zr, zl = lax.rem(z + 1, NZ), lax.rem(z + NZ - 1, NZ)

    def ring(v, k):
        return lax.rem(v + k, 4)

    def place(px, py, pc):
        return (px * NY + py) * NC + pc

    partner = place(x, y, d)
    x_peer = [place(ring(x, k), y, c) for k in (1, 2, 3)]
    y_peer = [place(x, ring(y, k), c) for k in (1, 2, 3)]
    a_peer = [place(ring(x, k * d), ring(y, k * c), c) for k in (1, 2, 3)]
    b_peer = [place(ring(x, k * c), ring(y, k * d), c) for k in (1, 2, 3)]

    here = [
        pltpu.make_async_copy(
            w_ref.at[p], wb.at[s, :, pl.ds(256 * p, 256)], lsem.at[p]
        )
        for p in range(3)
    ]
    here.append(pltpu.make_async_copy(tok_ref, tokb.at[z], lsem.at[3]))
    here.append(pltpu.make_async_copy(cot_ref, cotv, lsem.at[4]))
    here.append(pltpu.make_async_copy(ld_ref, ldv, lsem.at[5]))

    sent = []

    def send(src, dst, **dev):
        i = len(sent)
        copy = pltpu.make_async_remote_copy(
            src_ref=src, dst_ref=dst, send_sem=ssem.at[i], recv_sem=rsem.at[i],
            device_id=dev, device_id_type=MESH,
        )
        copy.start()
        sent.append((copy, None))
        return copy

    def send_if(needed, src, dst, peer):
        i = len(sent)
        copy = pltpu.make_async_remote_copy(
            src_ref=src, dst_ref=dst, send_sem=ssem.at[i], recv_sem=rsem.at[i],
            device_id={"seq": peer}, device_id_type=MESH,
        )
        pl.when(needed)(copy.start)
        sent.append((copy, needed))
        return copy

    here[3].start()
    for ref in (fa, fr, ba, br):
        ref[...] = jnp.zeros_like(ref)

    barrier = pltpu.get_barrier_semaphore()
    for peer in [partner] + x_peer + y_peer:
        pl.semaphore_signal(barrier, inc=1, device_id={"seq": peer}, device_id_type=MESH)
    for peer in (zr, zl):
        pl.semaphore_signal(barrier, inc=1, device_id={"dp": peer}, device_id_type=MESH)
    for copy in here[:3] + here[4:]:
        copy.start()
    pl.semaphore_wait(barrier, 9)

    first = (0, 1)
    way = (zr, zl)
    zc = {}
    here[3].wait()
    for h in (0, 1):
        for w in (0, 1):
            half = h if w == 0 else 1 - h
            zc[w, 0, half] = send(tokb.at[z, half], tokb.at[z, half], dp=way[w])
    for copy in here[:3]:
        copy.wait()
    wa = [send(wb.at[s], wb.at[s], seq=p) for p in a_peer]
    wp = [send(wb.at[s], wb.at[s], seq=partner)]

    here[5].wait()
    def decay_rows(i, total):
        h, b = lax.div(i, 4), lax.rem(i, 4)
        rows = pl.ds(pl.multiple_of(b * BLK, BLK), BLK)
        row_id = b * BLK + lax.broadcasted_iota(jnp.int32, (BLK, T), 0)
        col_id = lax.broadcasted_iota(jnp.int32, (BLK, T), 1)
        run = jnp.sum(jnp.where(col_id <= row_id, ldv[pl.ds(h, 1), :], 0.0), axis=1, keepdims=True)
        rc[h, rows, :] = jnp.broadcast_to(run, (BLK, BLK))
        return total

    lax.fori_loop(0, 8, decay_rows, 0)
    for h in range(HEADS):
        row = jnp.zeros((1, T), F32)
        for b in range(4):
            row_id = b * BLK + lax.broadcasted_iota(jnp.int32, (BLK, T), 0)
            col_id = lax.broadcasted_iota(jnp.int32, (BLK, T), 1)
            run = rc[h, b * BLK:(b + 1) * BLK, 0:1]
            row = row + jnp.sum(jnp.where(row_id == col_id, run, 0.0), axis=0, keepdims=True)
        rr[h] = row
        ttc[c, h] = rc[h, T - 8:T, :][7:8, :] + jnp.zeros((8, 128), F32)
    tc_copy = send(ttc.at[c], ttc.at[c], seq=partner)

    def mixing(i, zero):
        h, b = lax.div(i, 4), lax.rem(i, 4)
        rows = pl.ds(pl.multiple_of(b * BLK, BLK), BLK)
        row_id = b * BLK + lax.broadcasted_iota(jnp.int32, (BLK, T), 0)
        col_id = lax.broadcasted_iota(jnp.int32, (BLK, T), 1)
        spread = rc[h, rows, 0:1] - rr[h]
        mix[h, rows, :] = jnp.where(row_id >= col_id, jnp.exp(jnp.minimum(spread, 0.0)), 0.0)
        mixt[h, rows, :] = jnp.where(row_id <= col_id, jnp.exp(jnp.minimum(-spread, 0.0)), 0.0)
        lead[h, rows, :] = jnp.exp(rc[h, rows, :])
        fade[h, rows, :] = jnp.exp(ttc[c, h, 0:1, :] - rc[h, rows, :])
        return zero

    tc_copy.wait_recv()
    chip = x * NY + y
    tca[chip] = ttc[0] + ttc[1]
    ty_copy = [send(tca.at[chip], tca.at[chip], seq=p) for p in y_peer]

    for copy in wa:
        copy.wait_recv()
    wbc = []
    for k in (1, 2, 3):
        for m in range(4):
            src = place(m * d + x * c, y * d + m * c, c)
            wbc.append(send(wb.at[src], wb.at[src], seq=b_peer[k - 1]))
    for k in (1, 2, 3):
        src = place(ring(x, (4 - k) * d), ring(y, (4 - k) * c), c)
        wp.append(send(wb.at[src], wb.at[src], seq=partner))

    def pass_on(k):
        for half in (0, 1):
            for w in (0, 1):
                h = half if w == 0 else 1 - half
                if k == 3 and h != first[w]:
                    continue
                zc[w, k - 1, h].wait_recv()
                shard = lax.rem(z + (NZ - k if w == 0 else k), NZ)
                zc[w, k, h] = send(tokb.at[shard, h], tokb.at[shard, h], dp=way[w])

    def hand_over(k):
        for m in range(4):
            wbc[4 * (k - 1) + m].wait_recv()
        for m in range(4):
            back = 4 - k
            src = place(m * d + ring(x, back) * c, ring(y, back) * d + m * c, c)
            wp.append(send(wb.at[src], wb.at[src], seq=partner))

    pass_on(1)
    for copy in ty_copy:
        copy.wait_recv()
    line = pl.ds(NY * x, NY)
    tx_copy = [send(tca.at[line], tca.at[line], seq=p) for p in x_peer]
    lax.fori_loop(0, 8, mixing, 0)
    pass_on(2)
    hand_over(1)
    hand_over(3)
    for copy in tx_copy:
        copy.wait_recv()
    hand_over(2)

    def weigh(n, zero):
        k, i = lax.div(n, 4), lax.rem(n, 4)
        p = (x * d + i * c) * NY + i * d + y * c
        q = ring(x, k * d) * NY + ring(y, k * c)
        ahead = jnp.zeros((8, 128), F32)
        behind = jnp.zeros((8, 128), F32)
        for j in range(NX * NY):
            total = tca[j, c]
            ahead = ahead + jnp.logical_and(j > p, j < q).astype(F32) * total
            behind = behind + jnp.logical_and(j < p, j > q).astype(F32) * total
        wtf[n] = (p < q).astype(F32) * jnp.exp(ahead)
        wtb[n] = (p > q).astype(F32) * jnp.exp(behind)
        return zero

    lax.fori_loop(0, 16, weigh, 0)
    pass_on(3)
    here[4].wait()
    for copy in wp:
        copy.wait_recv()

    def weight_block(b):
        return wb[pl.ds(4 * b, 4)].reshape(T, 768)

    def project(b, start=False):
        part = mm(tokb[b].reshape(T, T), weight_block(b))
        if start:
            acc[...] = part
        else:
            acc[...] += part

    project(z, True)

    def project_near(i, zero):
        project(lax.rem(z + NZ - 2 + i + lax.div(i, 2), NZ))
        return zero

    lax.fori_loop(0, 4, project_near, 0)
    for w in (0, 1):
        zc[w, 2, 1 - first[w]].wait_recv()

    def project_far(i, zero):
        project(lax.rem(z + 3 + 2 * i, NZ))
        return zero

    lax.fori_loop(0, 2, project_far, 0)
    for w in (0, 1):
        zc[w, 3, first[w]].wait_recv()
    far = lax.rem(z + 4, NZ)
    acc[:, 256:768] += mm(
        tokb[far].reshape(T, T), wb[pl.ds(4 * far, 4), :, 256:768].reshape(T, 512)
    )

    def head(part, h):
        return pl.ds(pl.multiple_of(part * 256 + h * HD, HD), HD)

    def scalar(flag):
        return flag.astype(F32)

    t0, t1 = ttc[0, c, 0:1, :], ttc[1, c, 0:1, :]
    fc, fd = scalar(c), scalar(d)

    def mine(ref, j=None):
        return (ref[...] if j is None else ref[j]).astype(F32)

    def num(flag):
        return flag.astype(jnp.int32)

    def either(on0, on1):
        return d * on0 + c * on1 > 0

    forth, back = [[], []], [[], []]
    for k in (1, 2, 3):
        ty, tx, sy, sx = ring(y, k), ring(x, k), ring(y, 4 - k), ring(x, 4 - k)
        forth[0].append((
            either(num(x < 3) + num(ty > y), num(tx > x)),
            either(num(x < 3) + num(sy < y), num(sx < x)),
        ))
        on0, on1 = num(sx < x), num(x > 0) + num(sy < y)
        forth[1].append((
            either(num(tx > x), num(x > 0) + num(ty > y)), either(on0, on1), either(on1, on0)
        ))
        back[0].append((
            either(num(x > 0) + num(ty < y), num(tx < x)),
            either(num(x > 0) + num(sy > y), num(sx > x)),
        ))
        on0, on1 = num(sx > x), num(x < 3) + num(sy > y)
        back[1].append((
            either(num(tx < x), num(x < 3) + num(ty < y)), either(on0, on1), either(on1, on0)
        ))
    across = [place(ring(x, k * d), ring(y, k * c), d) for k in (1, 2, 3)]

    def exchange(needed, own, other, line, out, into, mid, entry, weights, wo, wp, f, side, fill, use):
        swap = send(own, other, seq=partner)
        fill[0]()
        swap.wait_recv()
        at = y * d + x * c
        line[at] = (wo * mine(own, c) + wp * mine(other, c)).astype(BF16)
        stage = [
            (send_if(needed[0][k][0], line.at[at], line.at[at], b_peer[k]), needed[0][k][1])
            for k in (1, 0, 2)
        ]
        fill[1]()
        for copy, there in stage:
            pl.when(there)(copy.wait_recv)

        def message(k):
            val = weights[4 * k, 0:1, :] * mine(line, 0)
            for i in (1, 2, 3):
                val = val + weights[4 * k + i, 0:1, :] * mine(line, i)
            return val

        near, far_side = [], []
        for k in (2, 1, 3):
            out[k] = message(k).astype(BF16)
            go, there, there_too = needed[1][k - 1]
            near.append((send_if(go, out.at[k], into.at[c, k], a_peer[k - 1]), there))
            far_side.append((send_if(go, out.at[k], into.at[c, k], across[k - 1]), there_too))
        mid[c] = message(0).astype(BF16)
        swap = send(mid.at[c], mid.at[c], seq=partner)
        fill[2]()

        def enter(h):
            total = mine(mid, h)
            for k in (1, 2, 3):
                total = total + into[h, k].astype(F32)
            total = jnp.exp(f * ttc[side, h, 0:1, :]) * total
            entry[h] = (total + f * mine(other, h)).astype(BF16)
            use(h)

        for copy, there in near:
            pl.when(there)(copy.wait_recv)
        enter(c)
        swap.wait_recv()
        for copy, there in far_side:
            pl.when(there)(copy.wait_recv)
        enter(d)

    act[:, 512:768] = acc[:, 512:768].astype(BF16)
    zk = acc[:, 256:512]
    act[:, 256:512] = (zk * sigmoid(zk)).astype(BF16)
    for h in range(HEADS):
        keys = act[:, head(1, h)].astype(F32) * fade[h]
        fs[h] = mm(keys.astype(BF16), act[:, head(2, h)], TN).astype(BF16)

    def queries():
        zq = acc[:, 0:256] + mm(
            tokb[far].reshape(T, T), wb[pl.ds(4 * far, 4), :, 0:256].reshape(T, 256)
        )
        acc[:, 0:256] = zq
        act[:, 0:256] = (zq * sigmoid(zq)).astype(BF16)

    def local_scores(h):
        q, k, v = (act[:, head(p, h)] for p in range(3))
        p = (mm(q, k, NT) * mix[h]).astype(BF16)
        inside[h] = mm(p, v)
        sc[h] = (mm(k, q, NT) * mixt[h]).astype(BF16)
        qlt[h] = (q.astype(F32) * lead[h]).T.astype(BF16)

    def attend(h):
        q = act[:, head(0, h)]
        attention = inside[h] + lead[h] * mm(q, fin[h])
        scale = jnp.sqrt(jnp.mean(attention * attention, axis=1, keepdims=True) + EPSILON)
        norm = attention / scale
        att_ref[:, head(0, h)] = norm.astype(BF16)
        up = cotv[:, head(0, h)].astype(F32)
        g = (up - norm * jnp.mean(up * norm, axis=1, keepdims=True)) / scale
        gout[h] = g.astype(BF16)
        bs[h] = mm(qlt[h], gout[h]).astype(BF16)

    exchange(
        forth, fs, fo, fa, fm, fr, fz, fin, wtf, jnp.exp(fd * t1), jnp.exp(fc * t1), fc, 0,
        (queries, lambda: local_scores(0), lambda: local_scores(1)), attend,
    )

    def local_grads(h):
        q, k, v = (act[:, head(p, h)] for p in range(3))
        g = gout[h]
        through = (mm(g, v, NT) * mix[h]).astype(BF16)
        gq = mm(through, k) + lead[h] * mm(g, fin[h], NT)
        zq = acc[:, head(0, h)]
        sg = sigmoid(zq)
        grad[:, head(0, h)] = (gq * (sg * (1.0 + zq * (1.0 - sg)))).astype(BF16)
        through = (mm(v, g, NT) * mixt[h]).astype(BF16)
        gkv[h] = mm(through, q)
        gkv[2 + h] = mm(sc[h], g)
        zk = acc[:, head(1, h)]
        sg = sigmoid(zk)
        acc[:, head(1, h)] = sg * (1.0 + zk * (1.0 - sg))

    def far_part(rows, columns):
        block = wb[pl.ds(4 * far, 4), :, columns]
        return mm(grad[rows, columns], block.reshape(T, block.shape[2]), NT)

    def far_queries():
        local_grads(1)
        for h in (0, 1):
            pbuf[far, h] = far_part(slice(h * HALF, (h + 1) * HALF), slice(0, 256))

    def last_grads(h):
        future = bin_[h]
        k, v = act[:, head(1, h)], act[:, head(2, h)]
        gk = gkv[h] + fade[h] * mm(v, future, NT)
        grad[:, head(1, h)] = (gk * acc[:, head(1, h)]).astype(BF16)
        grad[:, head(2, h)] = (gkv[2 + h] + fade[h] * mm(k, future)).astype(BF16)

    exchange(
        back, bs, bo, ba, bm, br, bz, bin_, wtb, jnp.exp(fc * t0), jnp.exp(fd * t0), fd, 1,
        (lambda: None, lambda: local_grads(0), far_queries), last_grads,
    )

    def token_part(b):
        pbuf[b] = mm(grad[...], weight_block(b), NT).reshape(2, HALF, T)

    bufs_s, bufs_r = (sr, sl), (rrv, rlv)
    gz = {}

    def block_at(w, k):
        return lax.rem(z + (4 - k if w == 0 else 4 + k), NZ)

    def send_sum(w, k, h):
        val = pbuf[block_at(w, k), h]
        if k > 0 and (w, k - 1, h) in gz:
            gz[w, k - 1, h].wait_recv()
            val = val + bufs_r[w][k - 1, h].astype(F32)
        bufs_s[w][k, h] = val.astype(BF16)
        gz[w, k, h] = send(bufs_s[w].at[k, h], bufs_r[w].at[k, h], dp=way[w])

    for h in (0, 1):
        rows = slice(h * HALF, (h + 1) * HALF)
        pbuf[far, h] += far_part(rows, slice(256, 768))
        send_sum(h, 0, h)

    def parts_far(i, zero):
        token_part(lax.rem(z + 3 + 2 * i, NZ))
        return zero

    lax.fori_loop(0, 2, parts_far, 0)
    send_sum(0, 1, 1)
    send_sum(1, 1, 0)

    def weight_part(b, zero):
        part = mm(tokb[b].reshape(T, T), grad[...], TN)
        pw[pl.ds(2 * b, 2)] = part.astype(BF16).reshape(2, 2, 128, 768)
        return zero

    gp = []
    for i in range(4):
        lax.fori_loop(2 * i, 2 * i + 2, weight_part, 0)
        gp.append(
            send(pw.at[4 * i:4 * i + 4, d], rpart.at[4 * i:4 * i + 4], seq=partner)
        )
    send_sum(0, 1, 0)
    send_sum(1, 1, 1)

    def chip_sum(i, zero):
        cs[i] = (pw[i, c].astype(F32) + rpart[i].astype(F32)).astype(BF16)
        return zero

    for i in range(4):
        gp[i].wait_recv()
        lax.fori_loop(4 * i, 4 * i + 4, chip_sum, 0)
    gb = []
    for k in (2, 1, 3):
        for m in range(4):
            src = (m * d + ring(x, k) * c) * NY + ring(y, k) * d + m * c
            gb.append(send(cs.at[src], rb.at[k - 1, m], seq=b_peer[k - 1]))

    def parts_near(i, zero):
        token_part(lax.rem(z + NZ - 2 + i, NZ))
        return zero

    lax.fori_loop(0, 5, parts_near, 0)
    send_sum(0, 2, 1)
    send_sum(1, 2, 0)
    send_sum(0, 2, 0)
    send_sum(1, 2, 1)
    send_sum(0, 3, 1)
    send_sum(1, 3, 0)
    send_sum(0, 3, 0)
    send_sum(1, 3, 1)
    for copy in gb:
        copy.wait_recv()
    for m in range(4):
        own = (m * d + x * c) * NY + y * d + m * c
        val = cs[own].astype(F32)
        for k in range(3):
            val = val + rb[k, m].astype(F32)
        dsum[m] = val.astype(BF16)
    at = x * d + y * c
    ga = [send(dsum.at[ring(at, k)], ra.at[k - 1], seq=a_peer[k - 1]) for k in (1, 2, 3)]
    for copy in ga:
        copy.wait_recv()
    val = dsum[at].astype(F32)
    for k in range(3):
        val = val + ra[k].astype(F32)
    val = (val * (1.0 / math.sqrt(16384.0))).astype(BF16)
    for p in range(3):
        gw_ref[p] = val[:, 256 * p:256 * (p + 1)]
    gz[0, 3, 1].wait_recv()
    gz[1, 3, 0].wait_recv()
    for h, ref in ((1, rrv), (0, rlv)):
        pbuf[z, h] += ref[3, h].astype(F32)
    gz[0, 3, 0].wait_recv()
    gz[1, 3, 1].wait_recv()
    for h, ref in ((0, rrv), (1, rlv)):
        gt_ref[h] = (pbuf[z, h] + ref[3, h].astype(F32)).astype(BF16)
    for copy, needed in sent:
        if needed is None:
            copy.wait_send()
        else:
            pl.when(needed)(copy.wait_send)
    assert len(sent) == COPIES, len(sent)


def hand_out(*refs):
    sems = refs[6]
    copies = [pltpu.make_async_copy(refs[i], refs[3 + i], sems.at[i]) for i in range(3)]
    for copy in copies:
        copy.start()
    for copy in copies:
        copy.wait()


def local(tokens, weights, log_decay, cotangent):
    vmem = pl.BlockSpec(memory_space=pltpu.VMEM)
    hbm = pl.BlockSpec(memory_space=pl.ANY)
    V = pltpu.VMEM
    states = [
        V((HEADS, HD, HD), BF16),
        V((HEADS, HD, HD), BF16),
        V((4, HD, HD), BF16),
        V((4, HD, HD), BF16), V((HEADS, 4, HD, HD), BF16),
        V((HEADS, HD, HD), BF16),
        V((HEADS, HD, HD), BF16),
    ]
    scratch = [
        V((NZ, 2, HALF, T), BF16),
        V((32, 128, 768), BF16),
        V((T, 256), BF16),
        V((HEADS, T), F32),
        V((T, 768), F32),
        V((T, 768), BF16),
        V((T, 768), BF16),
        V((HEADS, T, 128), F32),
        V((HEADS, 1, T), F32),
        V((HEADS, T, 128), F32), V((HEADS, T, 128), F32),
        V((HEADS, T, T), F32),
        V((HEADS, T, T), F32),
        V((HEADS, T, T), BF16),
        V((HEADS, T, HD), F32),
        V((HEADS, HD, T), BF16),
        V((HEADS, T, HD), BF16),
        V((4, T, HD), F32),
        V((2, HEADS, 8, 128), F32),
        V((16, HEADS, 8, 128), F32),
        V((16, 8, 128), F32), V((16, 8, 128), F32),
    ] + states + states + [
        V((NZ, 2, HALF, T), F32),
        V((4, 2, HALF, T), BF16), V((4, 2, HALF, T), BF16),
        V((4, 2, HALF, T), BF16), V((4, 2, HALF, T), BF16),
        V((16, 2, 128, 768), BF16),
        V((16, 128, 768), BF16),
        V((16, 128, 768), BF16),
        V((3, 4, 128, 768), BF16),
        V((4, 128, 768), BF16),
        V((3, 128, 768), BF16),
        pltpu.SemaphoreType.DMA((COPIES,)),
        pltpu.SemaphoreType.DMA((COPIES,)),
        pltpu.SemaphoreType.DMA((6,)),
    ]
    attended, grad_tokens, grad_weights = pl.pallas_call(
        kernel,
        out_shape=(
            pltpu.VMEM((T, 256), BF16),
            pltpu.VMEM((2, HALF, T), BF16),
            pltpu.VMEM((3, 128, 256), BF16),
        ),
        in_specs=[hbm] * 4,
        out_specs=(vmem,) * 3,
        scratch_shapes=scratch,
        compiler_params=pltpu.CompilerParams(
            collective_id=0, has_side_effects=True, vmem_limit_bytes=VMEM_LIMIT
        ),
        name="layer",
    )(tokens.reshape(2, HALF, T), weights.transpose(1, 0, 2), log_decay, cotangent)
    attended, grad_tokens, grad_weights = pl.pallas_call(
        hand_out,
        out_shape=(
            jax.ShapeDtypeStruct((T, 256), BF16),
            jax.ShapeDtypeStruct((2, HALF, T), BF16),
            jax.ShapeDtypeStruct((3, 128, 256), BF16),
        ),
        in_specs=[vmem] * 3,
        out_specs=(hbm,) * 3,
        scratch_shapes=[pltpu.SemaphoreType.DMA((3,))],
        compiler_params=pltpu.CompilerParams(vmem_limit_bytes=1 << 20),
        name="hand_out",
    )(attended, grad_tokens, grad_weights)
    return attended, grad_tokens.reshape(T, T), grad_weights.transpose(1, 0, 2)


def solution(mesh):
    return jax.shard_map(
        local,
        mesh=mesh,
        in_specs=(P("seq", "dp"), P("seq", None, "dp"), P("dp", "seq"), P("seq", "dp")),
        out_specs=(P("seq", "dp"), P("seq", "dp"), P("seq", None, "dp")),
        check_vma=False,
    )
```
